32 devices in a mesh: wide: 16 (over z, y, core), narrow: 2 (over x).
Axes of the slice: x: 2, y: 2, z: 4, core: 2. Of those that a mesh axis runs over, the one named last changes fastest.
Arguments:
- frames: bfloat16 [16384, 1024], P(('wide', 'narrow')), may hold values from -6 to 6
- segment_ids: int32 [16, 1024], P('wide', 'narrow'), may hold values from 0 to 3, never falling along the last dimension, each value on 1 to 512 neighbouring positions
- row_length: int32 [16], P('wide'), may hold values from 512 to 1024
- query_proj: bfloat16 [1024, 1024], P('wide', 'narrow'), may hold values from -0.1875 to 0.1875
- key_proj: bfloat16 [1024, 1024], P('wide', 'narrow'), may hold values from -0.1875 to 0.1875
- value_proj: bfloat16 [1024, 1024], P('wide', 'narrow'), may hold values from -0.1875 to 0.1875
- out_proj: bfloat16 [1024, 1024], P('wide', 'narrow'), may hold values from -0.375 to 0.375
- up_proj: bfloat16 [1024, 4096], P('wide', 'narrow'), may hold values from -0.1875 to 0.1875
- down_proj: bfloat16 [4096, 1024], P('wide', 'narrow'), may hold values from -0.09375 to 0.09375
- query_bias: bfloat16 [1024], P(('wide', 'narrow')), may hold values from -1.5 to 1.5
- value_bias: bfloat16 [1024], P(('wide', 'narrow')), may hold values from -1.5 to 1.5
- out_bias: bfloat16 [1024], P(('wide', 'narrow')), may hold values from -1.5 to 1.5
- up_bias: bfloat16 [4096], P(('wide', 'narrow')), may hold values from -1.5 to 1.5
- down_bias: bfloat16 [1024], P(('wide', 'narrow')), may hold values from -1.5 to 1.5
- attn_gain: bfloat16 [1024], P(('wide', 'narrow')), may hold values from 0.5 to 1.5
- mlp_gain: bfloat16 [1024], P(('wide', 'narrow')), may hold values from 0.5 to 1.5
- out_grad: bfloat16 [16384, 1024], P(('wide', 'narrow')), may hold values from -6 to 6
Outputs:
- block_out: bfloat16 [16384, 1024], P(('wide', 'narrow'))
- frames_grad: bfloat16 [16384, 1024], P(('wide', 'narrow'))
- query_proj_grad: float32 [1024, 1024], P('wide', 'narrow')
- key_proj_grad: float32 [1024, 1024], P('wide', 'narrow')
- value_proj_grad: float32 [1024, 1024], P('wide', 'narrow')
- out_proj_grad: float32 [1024, 1024], P('wide', 'narrow')
- up_proj_grad: float32 [1024, 4096], P('wide', 'narrow')
- down_proj_grad: float32 [4096, 1024], P('wide', 'narrow')
- query_bias_grad: float32 [1024], P(('wide', 'narrow'))
- value_bias_grad: float32 [1024], P(('wide', 'narrow'))
- out_bias_grad: float32 [1024], P(('wide', 'narrow'))
- up_bias_grad: float32 [4096], P(('wide', 'narrow'))
- down_bias_grad: float32 [1024], P(('wide', 'narrow'))
- attn_gain_grad: float32 [1024], P(('wide', 'narrow'))
- mlp_gain_grad: float32 [1024], P(('wide', 'narrow'))
The draws below stay inside these ranges and needn't reach their ends.
Inputs may be any that keep to these rules, and one draw needn't show every extreme that they name: `segment_ids`: segment numbers never fall along a row, and every one of the 4 numbers appears in each row.
All inputs are finite; a program needn't handle non-finite values.
Results may differ from the reference program's by a relative error of at most 0.018.
Values may be sent and summed in bfloat16 or wider, within the bound.
No kernel may reach another device: no remote copies, remote signals or barrier semaphores. Data moves between devices by JAX's collectives and lax.ppermute only.
A program may use at most 256 MiB of HBM per device.

```python
import math
import jax
import jax.numpy as jnp
import numpy as np
from jax import lax

D = 1024
HD = 64
FF = 4096
ROW_LEN = 1024
SEGS = 4
SEQS = 16
TOKENS = 16384


def touch_ends(result, rng, low, top_value):
    dims = result.shape
    place = [jax.random.randint(jax.random.fold_in(rng, axis), (), 0, dims[axis]) for axis in range(len(dims))]
    result = result.at[tuple(place)].set(low)
    longest = dims.index(max(dims))
    place[longest] = (place[longest] + 1) % dims[longest]
    return result.at[tuple(place)].set(top_value)


def with_spikes(drawn, key, source, target, shards_of, factor):
    def block_of(dim):
        return (jnp.arange(drawn.shape[dim]) // (drawn.shape[dim] // shards_of)).reshape((-1,) + (1,) * (drawn.ndim - 1 - dim))

    first = jax.random.permutation(key, shards_of)[block_of(target)]
    second = (block_of(target) + shards_of // 2) % shards_of
    return jnp.where((block_of(source) == first) | (block_of(source) == second), factor * drawn, drawn)


def shard_levels(own_key, dims, shards, smallest, top_value):
    loudness = 1.0
    for position, parts in shards:
        draws = jax.random.uniform(jax.random.fold_in(jax.random.fold_in(own_key, 6), position), (parts,), jnp.float32, smallest / len(shards), top_value / len(shards))
        loudness = loudness * jnp.repeat(jnp.exp(draws), dims[position] // parts).reshape((-1,) + (1,) * (len(dims) - 1 - position))
    return loudness


def length_profile(amount, total, limit, lean):
    weights = [(1 << 20) // math.isqrt(rank ** lean) + 1 for rank in range(2, amount + 1)]
    surplus, given = total - limit - (amount - 1), [1] * (amount - 1)
    while surplus > 0:
        movable = [i for i in range(amount - 1) if given[i] < limit]
        pool, remaining = sum([weights[i] for i in movable]), surplus
        for i in movable:
            more = min(limit - given[i], max(1, remaining * weights[i] // pool), surplus)
            given[i] = given[i] + more
            surplus = surplus - more
    return np.array([limit] + given)


def uneven_parts(stream_key, amount, total, most, skew):
    if amount == 2:
        one = jax.random.randint(stream_key, (), max(1, total - most), min(most, total - 1) + 1)
        return jnp.stack([one, total - one])
    tallies = jnp.asarray(length_profile(amount, total, most, skew), jnp.int32)
    couples = (amount - 1) // 2
    giver, taker = tallies[1:1 + 2 * couples:2], tallies[2:2 + 2 * couples:2]
    margin = jnp.minimum(giver - 1, most - taker)
    shifted = jax.random.randint(jax.random.fold_in(stream_key, 1), (couples,), 0, 1 << 20) % (margin + 1)
    tallies = tallies.at[1:1 + 2 * couples:2].set(giver - shifted).at[2:2 + 2 * couples:2].set(taker + shifted)
    return tallies[jax.random.permutation(jax.random.fold_in(stream_key, 2), amount)]


def scatter_about(stream_key, shape, scale, most, cuts=(), dtype=jnp.bfloat16):
    result = scale * jax.random.normal(stream_key, shape, jnp.float32)
    if cuts:
        result = result * shard_levels(stream_key, shape, cuts, -0.22, 0.18)
    return jnp.clip(result, -most, most).astype(dtype)


def bell_draw_with(stream_key, extent, width, bound, split, heavy, kind=jnp.bfloat16):
    array = width * jax.random.normal(stream_key, extent, jnp.float32)
    if split:
        array = array * shard_levels(stream_key, extent, split, -0.22, 0.18)
    return jnp.clip(with_spikes(array, jax.random.fold_in(stream_key, 3), *heavy), -bound, bound).astype(kind)


def setup_inputs(seed: int = 0) -> dict:
    seeds = jax.random.split(jax.random.key(seed), 18)
    return {
        "frames": scatter_about(seeds[0], (TOKENS, D), 1.0, 6.0, ((0, 32),)),
        "segment_ids": jax.vmap(lambda own: jnp.searchsorted(jnp.cumsum(uneven_parts(own, SEGS, ROW_LEN, ROW_LEN // 2, 0)), jnp.arange(ROW_LEN), side="right"))(jax.random.split(seeds[1], SEQS)).reshape((SEQS, ROW_LEN)).astype(jnp.int32),
        "row_length": touch_ends(jax.random.randint(seeds[2], (SEQS,), ROW_LEN // 2, ROW_LEN + 1), jax.random.fold_in(seeds[2], 1), ROW_LEN // 2, ROW_LEN).astype(jnp.int32),
        "query_proj": scatter_about(seeds[3], (D, D), D ** -0.5, 0.1875, ((0, 16), (1, 2))),
        "key_proj": scatter_about(seeds[4], (D, D), D ** -0.5, 0.1875, ((0, 16), (1, 2))),
        "value_proj": scatter_about(seeds[5], (D, D), D ** -0.5, 0.1875, ((0, 16), (1, 2))),
        "out_proj": scatter_about(seeds[6], (D, D), (D // 4) ** -0.5, 0.375, ((0, 16), (1, 2))),
        "up_proj": scatter_about(seeds[7], (D, FF), D ** -0.5, 0.1875, ((0, 16), (1, 2))),
        "down_proj": scatter_about(seeds[8], (FF, D), FF ** -0.5, 0.09375, ((0, 16), (1, 2))),
        "query_bias": scatter_about(seeds[9], (D,), 0.3, 1.5, ((0, 32),)),
        "value_bias": scatter_about(seeds[10], (D,), 0.3, 1.5, ((0, 32),)),
        "out_bias": scatter_about(seeds[11], (D,), 0.3, 1.5, ((0, 32),)),
        "up_bias": scatter_about(seeds[12], (FF,), 0.3, 1.5, ((0, 32),)),
        "down_bias": scatter_about(seeds[13], (D,), 0.3, 1.5, ((0, 32),)),
        "attn_gain": jnp.clip(1.0 + 0.1 * jax.random.normal(seeds[14], (D,), jnp.float32), 0.5, 1.5).astype(jnp.bfloat16),
        "mlp_gain": jnp.clip(1.0 + 0.1 * jax.random.normal(seeds[15], (D,), jnp.float32), 0.5, 1.5).astype(jnp.bfloat16),
        "out_grad": bell_draw_with(seeds[16], (TOKENS, D), 1.0, 6.0, ((0, 32),), (0, 1, 32, 2.75)),
    }


EPS = 1e-05

@jax.custom_vjp
def low(v):
    return lax.optimization_barrier(v.astype(jnp.bfloat16)).astype(jnp.float32)

@jax.custom_vjp
def low_back(v):
    return v

def low_keep(v):
    return (low(v), None)

def low_pass(kept, grad):
    return (grad,)

def back_keep(v):
    return (v, None)

def back_low(kept, grad):
    return (low(grad),)
low.defvjp(low_keep, low_pass)
low_back.defvjp(back_keep, back_low)

def matmul(left, right):
    return jnp.dot(left, right, precision=lax.Precision.HIGHEST, preferred_element_type=jnp.float32)

def rms_scale(values, gain):
    return values * lax.rsqrt(lax.optimization_barrier(jnp.mean(values * values, axis=-1, keepdims=True)) + EPS) * gain

def one_head(items):
    query_head, key_head, value_head, allowed = items
    scale = 1.0 / math.sqrt(HD)
    scores = low_back(matmul(query_head, key_head.T) * scale)
    masked = jnp.where(allowed, scores, -1000000000.0)
    top = lax.optimization_barrier(jnp.max(masked, axis=-1, keepdims=True))
    expo = jnp.exp(masked - top)
    probs = expo / lax.optimization_barrier(jnp.sum(expo, axis=-1, keepdims=True))
    return matmul(low(probs), value_head)

def one_row(frow, srow, lrow, params):
    query_proj, key_proj, value_proj, out_proj, up_proj, down_proj, query_bias, value_bias, out_bias, up_bias, down_bias, attn_gain, mlp_gain = params
    act_one = low(rms_scale(frow, attn_gain))
    queries = low(low_back(matmul(act_one, query_proj) + query_bias))
    keys = low(low_back(matmul(act_one, key_proj)))
    values = low(low_back(matmul(act_one, value_proj) + value_bias))
    length = frow.shape[0]
    q3 = jnp.transpose(queries.reshape(length, -1, HD), (1, 0, 2))
    k3 = jnp.transpose(keys.reshape(length, -1, HD), (1, 0, 2))
    v3 = jnp.transpose(values.reshape(length, -1, HD), (1, 0, 2))
    rows = jnp.arange(length)[:, None]
    cols = jnp.arange(length)[None, :]
    allowed = (cols <= rows) & (srow[:, None] == srow[None, :]) & ((cols < lrow) | (cols == rows))
    masks = jnp.broadcast_to(allowed[None], (q3.shape[0], length, length))
    heads = lax.map(jax.checkpoint(one_head), (q3, k3, v3, masks))
    context = jnp.transpose(heads, (1, 0, 2)).reshape(length, -1)
    context = low(low_back(context))
    attn = low_back(matmul(context, out_proj) + out_bias)
    mid = frow + attn
    act_two = low(rms_scale(mid, mlp_gain))
    pre = low_back(matmul(act_two, up_proj) + up_bias)
    hidden = low(jax.nn.gelu(pre))
    branch = low_back(matmul(hidden, down_proj) + down_bias)
    return mid + branch

def reference(frames, segment_ids, row_length, query_proj, key_proj, value_proj, out_proj, up_proj, down_proj, query_bias, value_bias, out_bias, up_bias, down_bias, attn_gain, mlp_gain, out_grad):
    inputs = [frames.astype(jnp.float32)] + [item.astype(jnp.float32) for item in (query_proj, key_proj, value_proj, out_proj, up_proj, down_proj, query_bias, value_bias, out_bias, up_bias, down_bias, attn_gain, mlp_gain)]

    def forward(frames32, *params):
        grouped = frames32.reshape(-1, ROW_LEN, D)

        def step(carry, items):
            frow, srow, lrow = items
            return (carry, one_row(frow, srow, lrow, params))
        _, outputs = lax.scan(jax.checkpoint(step), jnp.zeros((), jnp.float32), (grouped, segment_ids, row_length))
        return outputs.reshape(-1, D)
    block_out, pullback = jax.vjp(forward, *inputs)
    grads = pullback(out_grad.astype(jnp.float32))
    return (block_out.astype(jnp.bfloat16), grads[0].astype(jnp.bfloat16), grads[1], grads[2], grads[3], grads[4], grads[5], grads[6], grads[7], grads[8], grads[9], grads[10], grads[11], grads[12], grads[13])
```

```python
import functools
import math

import jax
import jax.numpy as jnp
from jax import lax
from jax.experimental import pallas as pl
from jax.experimental.pallas import tpu as pltpu
from jax.sharding import PartitionSpec as P

HD = 64


EPS = 1e-05

F32 = jnp.float32
BF = jnp.bfloat16


def dot(left, right):
    return jnp.dot(left, right, preferred_element_type=F32)


def dot_last(left, right):
    return lax.dot_general(left, right, (((1,), (1,)), ((), ())), preferred_element_type=F32)


def dot_first(left, right):
    return lax.dot_general(left, right, (((0,), (0,)), ((), ())), preferred_element_type=F32)


def ds(start, size):
    return pl.ds(pl.multiple_of(start, size), size)


def place(sc, p, nz, ny):
    zrel, yrel = p % nz, p // nz
    return lax.rem(sc[0] + nz - zrel, nz) * ny + lax.rem(sc[1] + ny - yrel, ny)


def call(kernel, sc, args, grid, in_specs, out_specs, out_shape, scratch=()):
    spec = pltpu.PrefetchScalarGridSpec(
        num_scalar_prefetch=1,
        grid=grid,
        in_specs=in_specs,
        out_specs=out_specs,
        scratch_shapes=list(scratch),
    )
    return pl.pallas_call(
        kernel,
        grid_spec=spec,
        out_shape=out_shape,
        compiler_params=pltpu.CompilerParams(dimension_semantics=("arbitrary",) * len(grid)),
    )(sc, *args)


def whole(shape):
    return pl.BlockSpec(shape, lambda i, sc: (0,) * len(shape), pipeline_mode=pl.Buffered(1))


def sds(shape, dtype):
    return jax.ShapeDtypeStruct(shape, dtype)


def qkv_kernel(
    sc, own, oth, gain, qb, vb, wa0, wa1, wb0, wb1, q_o, k_o, v_o, a_o, tmp, *, nz, ny, blk, grp
):
    i = pl.program_id(0)
    half = pl.num_programs(0) // 2
    mine = i // half == sc[3]
    f = jnp.where(mine, own[...].astype(F32), oth[...].astype(F32))
    r = lax.rsqrt(jnp.mean(f * f, axis=1, keepdims=True) + EPS)
    tmp[...] = (f * r * gain[...]).astype(BF)
    for p in range(nz * ny):
        a_o[:, p * blk : (p + 1) * blk] = tmp[:, ds(place(sc, p, nz, ny) * blk, blk)]
    k = nz * blk
    for g, (w0, w1) in enumerate(((wa0, wa1), (wb0, wb1))):
        res = dot(a_o[:, :k], w0[...].reshape(k, 3 * grp))
        res = res + dot(a_o[:, k:], w1[...].reshape(k, 3 * grp))
        lo, hi = g * grp, (g + 1) * grp
        q_o[:, lo:hi] = (res[:, :grp] + qb[:, lo:hi]).astype(BF)
        k_o[:, lo:hi] = res[:, grp : 2 * grp].astype(BF)
        v_o[:, lo:hi] = (res[:, 2 * grp :] + vb[:, lo:hi]).astype(BF)


def fill_bias(sc, segc, segr, bias, qb):
    total = bias.shape[0]
    for start in range(0, total, qb):
        n = start + qb
        rows = start + lax.broadcasted_iota(jnp.int32, (qb, n), 0)
        cols = lax.broadcasted_iota(jnp.int32, (qb, n), 1)
        ok = (cols <= rows) & (segc[start:n, :] == segr[:, :n])
        ok = ok & ((cols < sc[4]) | (cols == rows))
        bias[start:n, :n] = jnp.where(ok, 0.0, -1000000000.0)


def attn_kernel(sc, segc, segr, q, k, v, c_o, l_o, bias, *, qb):
    p = pl.program_id(0)
    total = q.shape[0]

    @pl.when(p == 0)
    def _():
        fill_bias(sc, segc, segr, bias, qb)
        l_o[...] = jnp.zeros_like(l_o)

    lane = lax.broadcasted_iota(jnp.int32, (qb, 128), 1)
    for start in range(0, total, qb):
        n = start + qb
        outs = []
        lse = l_o[start:n, :]
        for h in range(2):
            lo, hi = h * HD, (h + 1) * HD
            qh = q[start:n, lo:hi] * jnp.asarray(1.0 / math.sqrt(HD), BF)
            s = dot_last(qh, k[:n, lo:hi]) + bias[start:n, :n]
            top = jnp.max(s, axis=1, keepdims=True)
            e = jnp.exp(s - top)
            t = jnp.sum(e, axis=1, keepdims=True)
            pr = (e * (1.0 / t)).astype(BF)
            outs.append(dot(pr, v[:n, lo:hi]))
            lse = jnp.where(lane == 2 * p + h, top + jnp.log(t), lse)
        l_o[start:n, :] = lse
        c_o[start:n, :] = jnp.concatenate(outs, axis=1).astype(BF)


def attn_back_kernel(sc, segc, segr, q, k, v, d, l, dq_o, dk_o, dv_o, bias, dks, dvs, *, qb):
    p = pl.program_id(0)
    total = q.shape[0]

    @pl.when(p == 0)
    def _():
        fill_bias(sc, segc, segr, bias, qb)

    lane = lax.broadcasted_iota(jnp.int32, (qb, 128), 1)
    scale = jnp.asarray(1.0 / math.sqrt(HD), BF)
    for start in range(total - qb, -1, -qb):
        n = start + qb
        dqs, dkk, dvv = [], [], []
        for h in range(2):
            lo, hi = h * HD, (h + 1) * HD
            qh = q[start:n, lo:hi] * scale
            kh, vh, dh = k[:n, lo:hi], v[:n, lo:hi], d[start:n, lo:hi]
            lse = jnp.sum(jnp.where(lane == 2 * p + h, l[start:n, :], 0.0), axis=1, keepdims=True)
            pr = jnp.exp(dot_last(qh, kh) + bias[start:n, :n] - lse)
            dp = dot_last(dh, vh)
            inner = jnp.sum(pr * dp, axis=1, keepdims=True)
            dsc = (pr * (dp - inner)).astype(BF)
            dqs.append(dot(dsc, kh) * (1.0 / math.sqrt(HD)))
            dkk.append(dot_first(dsc, qh))
            dvv.append(dot_first(pr.astype(BF), dh))
        dq_o[start:n, :] = jnp.concatenate(dqs, axis=1).astype(BF)
        dkk, dvv = jnp.concatenate(dkk, axis=1), jnp.concatenate(dvv, axis=1)
        if n == total:
            dks[...] = dkk
            dvs[...] = dvv
        else:
            dks[:n, :] += dkk
            dvs[:n, :] += dvv
    dk_o[...] = dks[...].astype(BF)
    dv_o[...] = dvs[...].astype(BF)


def out_weight(wa, wb, xrel, crel, yrel):
    block = wa[yrel][:, xrel] if crel == 0 else wb[yrel, :, xrel]
    return block.reshape(block.shape[0] * block.shape[1], block.shape[2])


def out_kernel(
    sc, cown, coth, fr, ob, gain, wa0, wa1, wb, cr_o, mid_o, a_o, cs, ms, *, nz, ny, nx, blk, wc
):
    hw = cown.shape[1]
    x, c = sc[3], sc[2]
    cs[:, ds(x * hw, hw)] = cown[...]
    cs[:, ds((1 - x) * hw, hw)] = coth[...]
    for p in range(nz * ny):
        cr_o[:, p * blk : (p + 1) * blk] = cs[:, ds(place(sc, p, nz, ny) * blk, blk)]
    k = nz * blk
    for xrel in range(nx):
        for crel in range(2):
            acc = dot(cr_o[:, :k], out_weight((wa0, wa1), wb, xrel, crel, 0))
            acc = acc + dot(cr_o[:, k:], out_weight((wa0, wa1), wb, xrel, crel, 1))
            base = lax.rem(x + xrel, nx) * 2 + lax.rem(c + crel, 2)
            ms[:, ds(base * wc, wc)] = acc
    mid = fr[...].astype(F32) + ms[...] + ob[...]
    mid_o[...] = mid
    r = lax.rsqrt(jnp.mean(mid * mid, axis=1, keepdims=True) + EPS)
    cs[...] = (mid * r * gain[...]).astype(BF)
    for p in range(nz * ny):
        a_o[:, p * blk : (p + 1) * blk] = cs[:, ds(place(sc, p, nz, ny) * blk, blk)]


def mlp_kernel(
    sc, a0, a1, d0, d1, ub, up0, up1, dn0, dn1,
    bo_o, bs_o, da_o, ds_o, uo_o, us_o, do_o, dos_o, ug_o,
    act, act_t, dr, bacc, dacc,
):
    t = pl.program_id(0)
    m = a0.shape[0]
    hw = dn0.shape[3]
    x = sc[3]

    @pl.when(t == 0)
    def _():
        for row, (a, d) in enumerate(((a0, d0), (a1, d1))):
            act[row * m : (row + 1) * m, :] = a[...]
            act_t[:, row * m : (row + 1) * m] = a[...].T
            dr[row * m : (row + 1) * m, :hw] = d[:, ds(x * hw, hw)]
            dr[row * m : (row + 1) * m, hw:] = d[:, ds((1 - x) * hw, hw)]
        bacc[...] = jnp.zeros_like(bacc)
        dacc[...] = jnp.zeros_like(dacc)

    nz, ff = up0.shape[0], up0.shape[3]
    k = nz * up0.shape[2]
    u0 = up0[...].reshape(k, ff)
    u1 = up1[...].reshape(k, ff)
    w0 = dn0[...].reshape(ff, hw)
    w1 = dn1[...].reshape(ff, hw)
    pre = dot(act[:, :k], u0) + dot(act[:, k:], u1) + ub[...].reshape(1, ff)
    dh = dot_last(dr[:, :hw], w0) + dot_last(dr[:, hw:], w1)
    sq = pre * pre
    th = jnp.tanh(pre * (0.7978845608 + (0.7978845608 * 0.044715) * sq))
    hp = 0.5 * (1.0 + th)
    hid = (pre * hp).astype(BF)
    slope = hp + (0.5 * pre) * (1.0 - th * th) * (
        0.7978845608 + (3.0 * 0.7978845608 * 0.044715) * sq
    )
    dpre = (dh * slope).astype(BF)
    bacc[:, :hw] += dot(hid, w0)
    bacc[:, hw:] += dot(hid, w1)
    dacc[:, :k] += dot_last(dpre, u0)
    dacc[:, k:] += dot_last(dpre, u1)
    uo_o[...] = dot(act_t[:k, :], dpre).astype(BF).reshape(1, k, ff)
    us_o[...] = dot(act_t[k:, :], dpre).astype(BF).reshape(1, k, ff)
    hid_t = hid.T
    do_o[...] = dot(hid_t, dr[:, :hw]).astype(BF).reshape(1, ff, hw)
    dos_o[...] = dot(hid_t, dr[:, hw:]).astype(BF).reshape(1, ff, hw)
    ug_o[...] = jnp.sum(dpre.astype(F32), axis=0, keepdims=True).reshape(1, 1, ff)

    @pl.when(t == pl.num_programs(0) - 1)
    def _():
        bo_o[...] = bacc[:m, :]
        bs_o[...] = bacc[m:, :].astype(BF)
        da_o[...] = dacc[:m, :]
        ds_o[...] = dacc[m:, :].astype(BF)


def mid_kernel(
    sc, da, dr, bo, br, mid, do, gain, db, cr, wa0, wa1, wb,
    blk_o, dmid_o, dco_o, dcs_o, wo_o, ws_o, vec_o,
    tmp, dat, dcx, acc_o, acc_s, *, nz, ny, nx, blk, wc,
):
    i = pl.program_id(0)
    x, c = sc[3], sc[2]
    hw = bo.shape[1] // nx

    @pl.when(i == 0)
    def _():
        vec_o[...] = jnp.zeros_like(vec_o)
        acc_o[...] = jnp.zeros_like(acc_o)
        acc_s[...] = jnp.zeros_like(acc_s)

    mv = mid[...]
    for xrel in range(nx):
        part = bo[:, xrel * hw : (xrel + 1) * hw] + br[:, xrel * hw : (xrel + 1) * hw].astype(F32)
        tmp[:, ds(lax.rem(x + xrel, nx) * hw, hw)] = part
    blk_o[...] = (mv + tmp[...] + db[...]).astype(BF)
    for p in range(nz * ny):
        part = da[:, p * blk : (p + 1) * blk] + dr[:, p * blk : (p + 1) * blk].astype(F32)
        tmp[:, ds(place(sc, p, nz, ny) * blk, blk)] = part
    dact = tmp[...]
    r = lax.rsqrt(jnp.mean(mv * mv, axis=1, keepdims=True) + EPS)
    n = mv * r
    dn = dact * gain[...]
    dout = do[...].astype(F32)
    dmid = dout + r * (dn - n * jnp.mean(dn * n, axis=1, keepdims=True))
    dmid_o[...] = dmid
    dattn = dmid.astype(BF)
    dat[...] = dattn
    vec_o[0:1, :] += jnp.sum(dact * n, axis=0, keepdims=True)
    vec_o[1:2, :] += jnp.sum(dattn.astype(F32), axis=0, keepdims=True)
    vec_o[2:3, :] += jnp.sum(dout, axis=0, keepdims=True)
    k = nz * blk
    sums = [None, None]
    crt = cr[...].T
    for xrel in range(nx):
        for crel in range(2):
            base = lax.rem(x + xrel, nx) * 2 + lax.rem(c + crel, 2)
            piece = dat[:, ds(base * wc, wc)]
            for yrel in range(2):
                got = dot_last(piece, out_weight((wa0, wa1), wb, xrel, crel, yrel))
                sums[yrel] = got if sums[yrel] is None else sums[yrel] + got
            acc = acc_o if crel == 0 else acc_s
            acc[:, xrel * wc : (xrel + 1) * wc] += dot(crt, piece)
    for p in range(nz * ny):
        part = sums[p // nz][:, (p % nz) * blk : (p % nz + 1) * blk]
        dcx[:, ds(place(sc, p, nz, ny) * blk, blk)] = part.astype(BF)
    heads = dco_o.shape[1]
    dco_o[...] = dcx[:, ds(x * heads, heads)]
    dcs_o[...] = dcx[:, ds((1 - x) * heads, heads)]

    @pl.when(i == pl.num_programs(0) - 1)
    def _():
        wo_o[...] = acc_o[...].astype(BF)
        ws_o[...] = acc_s[...].astype(BF)


def dact_kernel(
    sc, dq, dk, dv, own, oth, gain, ar, wa0, wa1, wb0, wb1,
    da_o, ds_o, wo_o, ws_o, vec_o, tmp, acc, *, nz, ny, blk, grp,
):
    i = pl.program_id(0)
    half = pl.num_programs(0) // 2

    @pl.when(i == 0)
    def _():
        vec_o[...] = jnp.zeros_like(vec_o)
        acc[...] = jnp.zeros_like(acc)

    mine = i >= half
    f = jnp.where(mine, own[...].astype(F32), oth[...].astype(F32))
    r = lax.rsqrt(jnp.mean(f * f, axis=1, keepdims=True) + EPS)
    k = nz * blk
    sums = [None, None]
    art = ar[...].T
    for g, pair in enumerate(((wa0, wa1), (wb0, wb1))):
        lo, hi = g * grp, (g + 1) * grp
        cat = jnp.concatenate([dq[:, lo:hi], dk[:, lo:hi], dv[:, lo:hi]], axis=1)
        for yrel in range(2):
            got = dot_last(cat, pair[yrel][...].reshape(k, 3 * grp))
            sums[yrel] = got if sums[yrel] is None else sums[yrel] + got
        acc[:, g * 3 * grp : (g + 1) * 3 * grp] += dot(art, cat)
    for p in range(nz * ny):
        part = sums[p // nz][:, (p % nz) * blk : (p % nz + 1) * blk]
        tmp[:, ds(place(sc, p, nz, ny) * blk, blk)] = part
    dact = tmp[...]
    vec_o[0:1, :] += jnp.sum(dact * (f * r), axis=0, keepdims=True)
    w = 2 * grp
    vec_o[1:2, :w] += jnp.sum(dq[...].astype(F32), axis=0, keepdims=True)
    vec_o[2:3, :w] += jnp.sum(dv[...].astype(F32), axis=0, keepdims=True)

    @pl.when(mine)
    def _():
        da_o[...] = dact

    @pl.when(i < half)
    def _():
        ds_o[...] = dact.astype(BF)

    @pl.when(i == pl.num_programs(0) - 1)
    def _():
        wo_o[...] = acc[:, : 3 * grp].astype(BF)
        ws_o[...] = acc[:, 3 * grp :].astype(BF)


def last_kernel(sc, da, dr, dmid, fr, gain, o):
    f = fr[...].astype(F32)
    r = lax.rsqrt(jnp.mean(f * f, axis=1, keepdims=True) + EPS)
    n = f * r
    dn = (da[...] + dr[...].astype(F32)) * gain[...]
    o[...] = (dmid[...] + r * (dn - n * jnp.mean(dn * n, axis=1, keepdims=True))).astype(BF)


def add_low(*parts):
    total = parts[0].astype(F32)
    for part in parts[1:]:
        total = total + part.astype(F32)
    return total


def fast_body(nz, ny, nx, *args):
    (
        frames, segment_ids, row_length, query_proj, key_proj, value_proj, out_proj, up_proj,
        down_proj, query_bias, value_bias, out_bias, up_bias, down_bias, attn_gain, mlp_gain,
        out_grad,
    ) = args
    nw = nz * ny * 2
    nb = nz * ny
    w = lax.axis_index("wide")
    x = lax.axis_index("narrow")
    c = lax.rem(w, 2)
    y = lax.rem(w // 2, ny)
    z = w // (2 * ny)
    m, d = frames.shape
    rows = m * nx
    blk = d // nb
    grp = query_proj.shape[1] // 2
    wr = query_proj.shape[0]
    ffb = down_proj.shape[0]
    ffx = up_proj.shape[1] // 2
    nj = ffx // ffb
    wc = grp
    hw = d // nx

    def send_w(a, dz=0, dy=0, dc=0):
        perm = []
        for i in range(nw):
            zi, yi, ci = i // (2 * ny), (i // 2) % ny, i % 2
            perm.append((i, (((zi + dz) % nz) * ny + (yi + dy) % ny) * 2 + (ci + dc) % 2))
        return lax.ppermute(a, "wide", perm)

    def send_x(a, k=1):
        return lax.ppermute(a, "narrow", [(i, (i + k) % nx) for i in range(nx)])

    def send_xc(a):
        perm = []
        for i in range(nw):
            for j in range(nx):
                perm.append((i * nx + j, (i ^ 1) * nx + (j + 1) % nx))
        return lax.ppermute(a, ("wide", "narrow"), perm)

    send = {
        "z": lambda a, k: send_w(a, dz=k),
        "y": lambda a, k: send_w(a, dy=k),
        "x": lambda a, k: send_x(a, k),
    }
    size = {"z": nz, "y": ny, "x": nx}

    def gather(a, order):
        for at, dim in enumerate(order):
            parts = [a] + [send[dim](a, k) for k in range(1, size[dim])]
            if at == len(order) - 1:
                return parts
            a = jnp.stack(parts)

    def pick(flag, a, b):
        return jnp.where(flag == 0, a, b)

    def in_order(flag, own, oth, axis=0):
        return pick(
            flag, jnp.concatenate([own, oth], axis=axis), jnp.concatenate([oth, own], axis=axis)
        )

    vectors = (query_bias, value_bias, out_bias, up_bias, down_bias, attn_gain, mlp_gain)
    widths = [piece.shape[0] for piece in vectors]
    packed = jnp.concatenate(vectors)
    nv = packed.shape[0]
    segs = segment_ids[0]
    vec_x = send_x(jnp.concatenate([packed, segs.astype(BF)]))
    vec_xc = send_xc(packed)

    def halves(a):
        return a[:, :grp], a[:, grp:]

    up4 = up_proj.reshape(wr, nj, 2, ffb)
    qs, ks, vs, os = halves(query_proj), halves(key_proj), halves(value_proj), halves(out_proj)
    us = (up4[:, :, 0].reshape(wr, ffx), up4[:, :, 1].reshape(wr, ffx))
    sides = [jnp.concatenate([us[s], os[s], qs[s], ks[s], vs[s]], axis=1) for s in range(2)]
    keep = pick(c, sides[0], sides[1])
    give = pick(c, sides[1], sides[0])
    got = send_w(give, dc=1)
    vec_c = send_w(packed, dc=1)
    pair = in_order(c, keep, got)
    uo = pair[:, : ffx + grp]
    own_vec = in_order(x, packed[None], vec_x[None, :nv])
    oth_vec = in_order(x, vec_c[None], vec_xc[None])
    vec4 = in_order(c, own_vec, oth_vec).reshape(-1)
    tail_rows = 16
    vec_block = jnp.pad(vec4, (0, tail_rows * 3 * grp - vec4.shape[0])).reshape(tail_rows, 3 * grp)
    qkv_block = jnp.concatenate([pair[:, ffx + grp :], vec_block], axis=0)

    wa = gather(qkv_block, "zy")
    frames_oth = send_x(frames)
    wb = [send_w(a[:, : 2 * wr], dc=1) for a in wa]
    dout_par = send_w(out_grad, dc=1)
    uo_all = gather(uo, "xzy")
    down_all = gather(down_proj, "zyx")
    wo_par = send_w(jnp.stack([a[:, :, :, ffx:] for a in uo_all]), dc=1)

    count = nw * nx * nv // nb
    table = jnp.stack([a[:, 2 * wr :].reshape(nz, -1)[:, :count] for a in wa]).reshape(nb, count)
    here = jnp.arange(nb)
    back = lax.rem(y + ny - here % ny, ny) * nz + lax.rem(z + nz - here // ny, nz)
    table = dot((back[:, None] == here[None, :]).astype(BF), table).reshape(nw * nx, nv)
    full_vec = []
    offset = 0
    for width in widths:
        full_vec.append(table[:, offset : offset + width].reshape(1, -1))
        offset = offset + width
    b_query, b_value, b_out, b_up, b_down, g_attn, g_mlp = full_vec

    def own_heads(v):
        mine = lax.dynamic_slice(v, (0, x * 2 * grp), (1, 2 * grp))
        return pick(c, mine, jnp.concatenate([mine[:, grp:], mine[:, :grp]], axis=1))

    qb, vb = own_heads(b_query), own_heads(b_value)
    ub = lax.dynamic_index_in_dim(b_up.reshape(nb, 2, ffb), c, axis=1)

    sc_at = jnp.arange(5, dtype=jnp.int32)
    sc = jnp.where(sc_at == 0, z, jnp.where(sc_at == 1, y, jnp.where(sc_at == 2, c, x)))
    sc = jnp.where(sc_at == 4, row_length[0], sc).astype(jnp.int32)

    seg_row = in_order(x, segs, vec_x[nv:].astype(jnp.int32))
    segc, segr = seg_row.reshape(rows, 1), seg_row.reshape(1, rows)

    rb = min(256, m)
    steps = rows // rb
    per = m // rb
    wspec = whole((nz, 2 * wr, 3 * grp))
    dims = dict(nz=nz, ny=ny, blk=blk)
    row_own = pl.BlockSpec((rb, d), lambda i, sc: (i % per, 0))
    wide_row = pl.BlockSpec((rb, d), lambda i, sc: (i, 0))
    heads_row = pl.BlockSpec((rb, 2 * grp), lambda i, sc: (i, 0))
    q, k, v, act_one = call(
        functools.partial(qkv_kernel, grp=grp, **dims),
        sc,
        (frames, frames_oth, g_attn, qb, vb, wa[0], wa[1], wb[0], wb[1]),
        (steps,),
        [row_own, row_own, whole((1, d)), whole((1, 2 * grp)), whole((1, 2 * grp))] + [wspec] * 4,
        [heads_row, heads_row, heads_row, wide_row],
        [sds((rows, 2 * grp), BF)] * 3 + [sds((rows, d), BF)],
        [pltpu.VMEM((rb, d), BF)],
    )

    pairs = 2 * grp // 128
    qblk = min(256, rows)
    rel_pair = pl.BlockSpec((rows, 128), lambda i, sc: (0, i))

    def abs_map(i, sc):
        return (0, lax.rem(i + sc[2] * (pairs // 2), pairs))

    abs_pair = pl.BlockSpec((rows, 128), abs_map)
    ctx, lse = call(
        functools.partial(attn_kernel, qb=qblk),
        sc,
        (segc, segr, q, k, v),
        (pairs,),
        [whole((rows, 1)), whole((1, rows)), rel_pair, rel_pair, rel_pair],
        [abs_pair, whole((rows, 128))],
        [sds((rows, 2 * grp), BF), sds((rows, 128), F32)],
        [pltpu.VMEM((rows, rows), F32)],
    )

    def split_rows(a):
        return (
            lax.dynamic_slice(a, (x * m, 0), (m, a.shape[1])),
            lax.dynamic_slice(a, ((1 - x) * m, 0), (m, a.shape[1])),
        )

    ctx_own, ctx_give = split_rows(ctx)
    ctx_oth = send_x(ctx_give)

    ospec = pl.BlockSpec(
        (nz, nx, blk, wc), lambda i, sc: (0, 0, 0, ffx // wc), pipeline_mode=pl.Buffered(1)
    )
    obspec = whole((2, nz, nx, blk, wc))
    fsteps = m // rb
    half_row = pl.BlockSpec((rb, 2 * grp), lambda i, sc: (i, 0))
    ctx_rel, mid, act_own = call(
        functools.partial(out_kernel, nx=nx, wc=wc, **dims),
        sc,
        (ctx_own, ctx_oth, frames, b_out, g_mlp, uo_all[0], uo_all[1], wo_par),
        (fsteps,),
        [half_row, half_row, wide_row, whole((1, d)), whole((1, d)), ospec, ospec, obspec],
        [wide_row, wide_row, wide_row],
        [sds((m, d), BF), sds((m, d), F32), sds((m, d), BF)],
        [pltpu.VMEM((rb, d), BF), pltpu.VMEM((rb, d), F32)],
    )
    act_par = send_w(act_own, dc=1)

    def up_map(t, sc):
        zy = place(sc, t, nz, ny)
        xrel = lax.rem(sc[3] + nx - zy // nj, nx)
        return xrel, zy % nj

    def up_in(t, sc):
        xrel, j = up_map(t, sc)
        return (0, xrel, 0, j)

    def up_out(t, sc):
        xrel, j = up_map(t, sc)
        return (xrel, 0, j)

    upspec = pl.BlockSpec((nz, 1, blk, ffb), up_in)
    dnspec = pl.BlockSpec((1, 1, ffb, hw), lambda t, sc: (t // nz, t % nz, 0, 0))
    bspec = pl.BlockSpec((1, 1, ffb), lambda t, sc: (place(sc, t, nz, ny), 0, 0))
    kk = nz * blk
    bo, bo_give, da, da_give, gu, gu_give, gd, gd_give, g_up = call(
        mlp_kernel,
        sc,
        (act_own, act_par, out_grad, dout_par, ub, uo_all[0], uo_all[1], down_all[0], down_all[1]),
        (nb,),
        [whole((m, d))] * 4 + [bspec, upspec, upspec, dnspec, dnspec],
        [whole((m, d))] * 4
        + [pl.BlockSpec((1, kk, ffb), up_out)] * 2
        + [pl.BlockSpec((1, ffb, hw), lambda t, sc: (t, 0, 0))] * 2
        + [bspec],
        [sds((m, d), F32), sds((m, d), BF), sds((m, d), F32), sds((m, d), BF)]
        + [sds((nx, kk, nj * ffb), BF)] * 2
        + [sds((nb, ffb, hw), BF)] * 2
        + [sds((nb, 1, ffb), F32)],
        [
            pltpu.VMEM((2 * m, d), BF),
            pltpu.VMEM((d, 2 * m), BF),
            pltpu.VMEM((2 * m, d), BF),
            pltpu.VMEM((2 * m, d), F32),
            pltpu.VMEM((2 * m, d), F32),
        ],
    )
    da_got = send_w(da_give, dc=1)
    bo_got = send_w(bo_give, dc=1)
    gd_got = send_x(gd_give)
    gu_got = send_w(gu_give, dy=1)

    gblk, dmid, dctx_own, dctx_give, wo, wo_give, vec_mid = call(
        functools.partial(mid_kernel, nx=nx, wc=wc, **dims),
        sc,
        (
            da, da_got, bo, bo_got, mid, out_grad, g_mlp, b_down, ctx_rel,
            uo_all[0], uo_all[1], wo_par,
        ),
        (fsteps,),
        [wide_row] * 6 + [whole((1, d)), whole((1, d)), wide_row, ospec, ospec, obspec],
        [wide_row, wide_row, half_row, half_row, whole((d, nx * wc)), whole((d, nx * wc))]
        + [whole((8, d))],
        [sds((m, d), BF), sds((m, d), F32), sds((m, 2 * grp), BF), sds((m, 2 * grp), BF)]
        + [sds((d, nx * wc), BF)] * 2
        + [sds((8, d), F32)],
        [
            pltpu.VMEM((rb, d), F32),
            pltpu.VMEM((rb, d), BF),
            pltpu.VMEM((rb, d), BF),
            pltpu.VMEM((d, nx * wc), F32),
            pltpu.VMEM((d, nx * wc), F32),
        ],
    )
    block_out = gblk
    dctx_oth = send_x(dctx_give)
    wo_got = send_w(wo_give, dc=1)
    dctx = in_order(x, dctx_own, dctx_oth)

    dq, dk, dv = call(
        functools.partial(attn_back_kernel, qb=qblk),
        sc,
        (segc, segr, q, k, v, dctx, lse),
        (pairs,),
        [whole((rows, 1)), whole((1, rows)), rel_pair, rel_pair, rel_pair, abs_pair]
        + [whole((rows, 128))],
        [rel_pair] * 3,
        [sds((rows, 2 * grp), BF)] * 3,
        [
            pltpu.VMEM((rows, rows), F32),
            pltpu.VMEM((rows, 128), F32),
            pltpu.VMEM((rows, 128), F32),
        ],
    )

    gd0 = [add_low(gd[e : e + nz], gd_got[e : e + nz]).astype(BF) for e in range(0, nb, nz)]
    gd1 = add_low(gd0[0], *[send_w(gd0[e], dy=-e) for e in range(1, ny)]).astype(BF)
    down_grad = add_low(gd1[0], *[send_w(gd1[e], dz=-e) for e in range(1, nz)])

    gu = gu.reshape(nx, nz, blk, ffx)
    gu_got = gu_got.reshape(nx, nz, blk, ffx)
    gu0 = [add_low(gu[:, e], gu_got[:, e]).astype(BF) for e in range(nz)]
    gu1 = add_low(gu0[0], *[send_w(gu0[e], dz=-e) for e in range(1, nz)]).astype(BF)
    gu2 = add_low(gu1[0], *[send_x(gu1[e], -e) for e in range(1, nx)])

    go0 = add_low(wo, wo_got).astype(BF)
    go1 = add_low(go0[:, :wc], send_x(go0[:, wc:])).reshape(nb, blk, wc)

    def abs_rows(i, sc):
        return (lax.rem(i + (1 - sc[3]) * per, 2 * per), 0)

    order_row = pl.BlockSpec((rb, 2 * grp), abs_rows)
    order_wide = pl.BlockSpec((rb, d), abs_rows)
    late = pl.BlockSpec((rb, d), lambda i, sc: (jnp.maximum(i - per, 0), 0))
    early = pl.BlockSpec((rb, d), lambda i, sc: (jnp.minimum(i, per - 1), 0))
    dact, dact_give, wg, wg_give, vec_one = call(
        functools.partial(dact_kernel, grp=grp, **dims),
        sc,
        (dq, dk, dv, frames, frames_oth, g_attn, act_one, wa[0], wa[1], wb[0], wb[1]),
        (steps,),
        [order_row] * 3 + [late, early, whole((1, d)), order_wide] + [wspec] * 4,
        [late, early, whole((d, 3 * grp)), whole((d, 3 * grp)), whole((8, d))],
        [sds((m, d), F32), sds((m, d), BF)] + [sds((d, 3 * grp), BF)] * 2 + [sds((8, d), F32)],
        [pltpu.VMEM((rb, d), F32), pltpu.VMEM((d, 6 * grp), F32)],
    )
    dact_got = send_x(dact_give)
    wg_got = send_w(wg_give, dc=1)

    def other_heads(v):
        mine = pick(c, v, jnp.concatenate([v[:, grp:], v[:, :grp]], axis=1))
        return in_order(x, mine, jnp.zeros_like(mine), axis=1)

    core_at = lax.broadcasted_iota(jnp.int32, (nb, 2, ffb), 1)
    up_bias_grad = jnp.where(core_at == c, g_up.reshape(nb, 1, ffb), 0.0)
    small = (
        other_heads(vec_one[1:2, : 2 * grp]),
        other_heads(vec_one[2:3, : 2 * grp]),
        vec_mid[1:2],
        up_bias_grad,
        vec_mid[2:3],
        vec_one[0:1],
        vec_mid[0:1],
    )
    vg = jnp.concatenate([g.reshape(nw * nx, width) for g, width in zip(small, widths)], axis=1)
    vg = vg + send_w(vg, dc=1)
    vg = vg + send_x(vg)
    vg = vg + sum(send_w(vg, dy=e) for e in range(1, ny))
    vg = vg + sum(send_w(vg, dz=e) for e in range(1, nz))
    flat = lax.dynamic_slice(vg, (w * nx + x, 0), (1, nv)).reshape(-1)
    vec_out = []
    offset = 0
    for width in widths:
        vec_out.append(flat[offset : offset + width])
        offset = offset + width

    gq0 = add_low(wg, wg_got).reshape(nb, blk, 3 * grp)
    gq0 = jnp.concatenate([gq0, go1], axis=2).astype(BF)
    gq1 = [gq0[e : e + nz] for e in range(0, nb, nz)]
    gq1 = add_low(gq1[0], *[send_w(gq1[e], dy=-e) for e in range(1, ny)]).astype(BF)
    gq2 = add_low(gq1[0], *[send_w(gq1[e], dz=-e) for e in range(1, nz)])

    last = jnp.concatenate([gu2, gq2], axis=1)
    mine = lax.dynamic_slice(last, (c * wr, 0), (wr, last.shape[1]))
    theirs = send_w(
        lax.dynamic_slice(last, ((1 - c) * wr, 0), (wr, last.shape[1])).astype(BF), dc=1
    ).astype(F32)
    sides = (pick(c, mine, theirs), pick(c, theirs, mine))
    up_grad = jnp.concatenate(
        [s[:, :ffx].reshape(wr, nj, 1, ffb) for s in sides], axis=2
    ).reshape(wr, 2 * ffx)
    weights = []
    for at in range(4):
        lo = ffx + at * grp
        weights.append(jnp.concatenate([s[:, lo : lo + grp] for s in sides], axis=1))

    rowspec = pl.BlockSpec((rb, d), lambda i, sc: (i, 0))
    frames_grad = call(
        last_kernel,
        sc,
        (dact, dact_got, dmid, frames, g_attn),
        (fsteps,),
        [rowspec] * 4 + [whole((1, d))],
        rowspec,
        sds((m, d), BF),
    )
    return (block_out, frames_grad, *weights, up_grad, down_grad, *vec_out)


def product(left, right):
    return jnp.dot(left, right, preferred_element_type=jnp.float32)


def contract_first(left, right):
    return lax.dot_general(
        left, right, (((0,), (0,)), ((), ())), preferred_element_type=jnp.float32
    )


def contract_last(left, right):
    return lax.dot_general(
        left, right, (((1,), (1,)), ((), ())), preferred_element_type=jnp.float32
    )


def rms_scale(values, gain):
    return values * lax.rsqrt(jnp.mean(values * values, axis=-1, keepdims=True) + EPS) * gain


def gather_params(shards):
    inner = (
        lax.all_gather(shards[0], "narrow", axis=1, tiled=True),
        lax.all_gather(shards[1], "narrow", axis=1, tiled=True),
        lax.all_gather(shards[2], "narrow", axis=1, tiled=True),
        lax.all_gather(shards[3], "narrow", axis=1, tiled=True),
        lax.all_gather(shards[4], "narrow", axis=1, tiled=True),
        lax.all_gather(shards[5], "narrow", axis=1, tiled=True),
        lax.all_gather(shards[6], "narrow", axis=1, tiled=True),
    )
    return (
        lax.all_gather(inner[0], "wide", axis=0, tiled=True),
        lax.all_gather(inner[1], "wide", axis=0, tiled=True),
        lax.all_gather(inner[2], "wide", axis=0, tiled=True),
        lax.all_gather(inner[3], "wide", axis=0, tiled=True),
        lax.all_gather(inner[4], "wide", axis=0, tiled=True),
        lax.all_gather(inner[5], "wide", axis=0, tiled=True),
        lax.all_gather(inner[6], "wide", axis=0, tiled=True),
    )


def gather_again(shards):
    inner = (
        lax.all_gather(shards[0], "narrow", axis=1, tiled=True),
        lax.all_gather(shards[1], "narrow", axis=1, tiled=True),
        lax.all_gather(shards[2], "narrow", axis=1, tiled=True),
        lax.all_gather(shards[3], "narrow", axis=1, tiled=True),
        lax.all_gather(shards[4], "narrow", axis=1, tiled=True),
        lax.all_gather(shards[5], "narrow", axis=1, tiled=True),
        lax.all_gather(shards[6], "narrow", axis=1, tiled=True),
    )
    return (
        lax.all_gather(inner[0], "wide", axis=0, tiled=True),
        lax.all_gather(inner[1], "wide", axis=0, tiled=True),
        lax.all_gather(inner[2], "wide", axis=0, tiled=True),
        lax.all_gather(inner[3], "wide", axis=0, tiled=True),
        lax.all_gather(inner[4], "wide", axis=0, tiled=True),
        lax.all_gather(inner[5], "wide", axis=0, tiled=True),
        lax.all_gather(inner[6], "wide", axis=0, tiled=True),
    )


def unpack_vectors(packed, widths):
    table = packed.reshape(-1, packed.shape[-1])
    pieces = []
    offset = 0
    for width in widths:
        pieces.append(table[:, offset : offset + width].reshape(-1).astype(jnp.float32))
        offset = offset + width
    return pieces


def build_mask(own_segments, row_segments, limit, offset, start, count):
    total = row_segments.shape[0]
    rows = offset + start + lax.broadcasted_iota(jnp.int32, (count, total), 0)
    cols = lax.broadcasted_iota(jnp.int32, (count, total), 1)
    same = own_segments[:, None] == row_segments[None, :]
    return (cols <= rows) & same & ((cols < limit) | (cols == rows))


def attend(query_part, key_part, value_part, allowed):
    scale = 1.0 / math.sqrt(HD)
    q3 = query_part.reshape(query_part.shape[0], -1, HD)
    k3 = key_part.reshape(key_part.shape[0], -1, HD)
    v3 = value_part.reshape(value_part.shape[0], -1, HD)
    scores = jnp.einsum("qhd,khd->hqk", q3, k3, preferred_element_type=jnp.float32) * scale
    masked = jnp.where(allowed[None], scores, -1000000000.0)
    top = jnp.max(masked, axis=-1, keepdims=True)
    expo = jnp.exp(masked - top)
    total = jnp.sum(expo, axis=-1, keepdims=True)
    probs = (expo / total).astype(jnp.bfloat16)
    context = jnp.einsum("hqk,khd->qhd", probs, v3, preferred_element_type=jnp.float32)
    return (context.reshape(query_part.shape[0], -1), top + jnp.log(total))


def attend_back(query_part, key_part, value_part, dctx_part, lse_part, allowed):
    scale = 1.0 / math.sqrt(HD)
    q3 = query_part.reshape(query_part.shape[0], -1, HD)
    k3 = key_part.reshape(key_part.shape[0], -1, HD)
    v3 = value_part.reshape(value_part.shape[0], -1, HD)
    d3 = dctx_part.reshape(dctx_part.shape[0], -1, HD)
    scores = jnp.einsum("qhd,khd->hqk", q3, k3, preferred_element_type=jnp.float32) * scale
    masked = jnp.where(allowed[None], scores, -1000000000.0)
    probs32 = jnp.exp(masked - lse_part)
    dprobs = jnp.einsum("qhd,khd->hqk", d3, v3, preferred_element_type=jnp.float32)
    inner = jnp.sum(probs32 * dprobs, axis=-1, keepdims=True)
    dscores = (probs32 * (dprobs - inner)).astype(jnp.bfloat16)
    dquery = jnp.einsum("hqk,khd->qhd", dscores, k3, preferred_element_type=jnp.float32) * scale
    dkey = jnp.einsum("hqk,qhd->khd", dscores, q3, preferred_element_type=jnp.float32) * scale
    dvalue = jnp.einsum(
        "hqk,qhd->khd", probs32.astype(jnp.bfloat16), d3, preferred_element_type=jnp.float32
    )
    return (
        dquery.reshape(query_part.shape[0], -1),
        dkey.reshape(key_part.shape[0], -1),
        dvalue.reshape(key_part.shape[0], -1),
    )


def body(
    frames,
    segment_ids,
    row_length,
    query_proj,
    key_proj,
    value_proj,
    out_proj,
    up_proj,
    down_proj,
    query_bias,
    value_bias,
    out_bias,
    up_bias,
    down_bias,
    attn_gain,
    mlp_gain,
    out_grad,
):
    vectors = (query_bias, value_bias, out_bias, up_bias, down_bias, attn_gain, mlp_gain)
    widths = [piece.shape[0] for piece in vectors]
    packed = jnp.concatenate(vectors).reshape(1, 1, -1)
    shards = (query_proj, key_proj, value_proj, out_proj, up_proj, down_proj, packed)
    full = gather_params(shards)
    w_query, w_key, w_value, w_out, w_up, w_down = (
        full[0],
        full[1],
        full[2],
        full[3],
        full[4],
        full[5],
    )
    b_query, b_value, b_out, b_up, b_down, g_attn, g_mlp = unpack_vectors(full[6], widths)
    length = frames.shape[0]
    own_segments = segment_ids[0]
    limit = row_length[0]
    offset = lax.axis_index("narrow") * length
    frames32 = frames.astype(jnp.float32)
    act_one = rms_scale(frames32, g_attn).astype(jnp.bfloat16)
    queries = (product(act_one, w_query) + b_query).astype(jnp.bfloat16)
    keys = product(act_one, w_key).astype(jnp.bfloat16)
    values = (product(act_one, w_value) + b_value).astype(jnp.bfloat16)
    row_parts = (
        lax.all_gather(keys, "narrow", axis=0, tiled=True),
        lax.all_gather(values, "narrow", axis=0, tiled=True),
        lax.all_gather(own_segments.astype(jnp.bfloat16), "narrow", axis=0, tiled=True),
    )
    row_keys, row_values = (row_parts[0], row_parts[1])
    row_segments = row_parts[2].astype(jnp.int32)
    total = row_keys.shape[0]
    block = min(length, 512)
    starts = list(range(0, length, block))
    masks = [
        build_mask(own_segments, row_segments, limit, offset, start, block) for start in starts
    ]
    width = queries.shape[1]
    group_width = 4 * HD
    firsts = list(range(0, width, group_width))
    context_cols = []
    lse_store = []
    for first in firsts:
        key_group = row_keys[:, first : first + group_width]
        value_group = row_values[:, first : first + group_width]
        pieces = []
        lse_group = []
        for index, start in enumerate(starts):
            piece, lse_part = attend(
                queries[start : start + block, first : first + group_width],
                key_group,
                value_group,
                masks[index],
            )
            pieces.append(piece)
            lse_group.append(lse_part)
        context_cols.append(pieces[0])
        lse_store.append(lse_group)
    context = jnp.concatenate(context_cols, axis=1).astype(jnp.bfloat16)
    mid = frames32 + product(context, w_out) + b_out
    act_two = rms_scale(mid, g_mlp).astype(jnp.bfloat16)
    pre = product(act_two, w_up) + b_up
    hidden = jax.nn.gelu(pre).astype(jnp.bfloat16)
    block_out = (mid + product(hidden, w_down) + b_down).astype(jnp.bfloat16)
    again = gather_again(shards)
    w_query, w_key, w_value, w_out, w_up, w_down = (
        again[0],
        again[1],
        again[2],
        again[3],
        again[4],
        again[5],
    )
    b_query, b_value, b_out, b_up, b_down, g_attn, g_mlp = unpack_vectors(again[6], widths)
    dout32 = out_grad.astype(jnp.float32)
    down_bias_grad = jnp.sum(dout32, axis=0)
    down_grad = contract_first(hidden, out_grad)
    dhidden = contract_last(out_grad, w_down)
    _, gelu_back = jax.vjp(jax.nn.gelu, pre)
    dpre = gelu_back(dhidden)[0].astype(jnp.bfloat16)
    up_bias_grad = jnp.sum(dpre.astype(jnp.float32), axis=0)
    up_grad = contract_first(act_two, dpre)
    dact_two = contract_last(dpre, w_up)
    _, norm_two_back = jax.vjp(rms_scale, mid, g_mlp)
    dmid_norm, mlp_gain_grad = norm_two_back(dact_two)
    dmid = dout32 + dmid_norm
    dattn = dmid.astype(jnp.bfloat16)
    out_bias_grad = jnp.sum(dattn.astype(jnp.float32), axis=0)
    out_grad_w = contract_first(context, dattn)
    dcontext = contract_last(dattn, w_out).astype(jnp.bfloat16)
    dquery_cols = []
    dkey_cols = []
    dvalue_cols = []
    for group_index, first in enumerate(firsts):
        key_group = row_keys[:, first : first + group_width]
        value_group = row_values[:, first : first + group_width]
        dkey_sum = jnp.zeros((total, group_width), jnp.float32)
        dvalue_sum = jnp.zeros((total, group_width), jnp.float32)
        dquery_parts = []
        for index, start in enumerate(starts):
            dquery, dkey, dvalue = attend_back(
                queries[start : start + block, first : first + group_width],
                key_group,
                value_group,
                dcontext[start : start + block, first : first + group_width],
                lse_store[group_index][index],
                masks[index],
            )
            dquery_parts.append(dquery)
            dkey_sum = dkey
            dvalue_sum = dvalue
        dquery_cols.append(dquery_parts[0])
        dkey_cols.append(dkey_sum)
        dvalue_cols.append(dvalue_sum)
    dqueries = jnp.concatenate(dquery_cols, axis=1).astype(jnp.bfloat16)
    dkey_row = jnp.concatenate(dkey_cols, axis=1)
    dvalue_row = jnp.concatenate(dvalue_cols, axis=1)
    own_parts = (
        lax.psum_scatter(
            dkey_row.astype(jnp.bfloat16), "narrow", scatter_dimension=0, tiled=True
        ).astype(jnp.float32),
        lax.psum_scatter(
            dvalue_row.astype(jnp.bfloat16), "narrow", scatter_dimension=0, tiled=True
        ).astype(jnp.float32),
    )
    dkeys = own_parts[0].astype(jnp.bfloat16)
    dvalues = own_parts[1].astype(jnp.bfloat16)
    query_bias_grad = jnp.sum(dqueries.astype(jnp.float32), axis=0)
    value_bias_grad = jnp.sum(dvalues.astype(jnp.float32), axis=0)
    query_grad = contract_first(act_one, dqueries)
    key_grad = contract_first(act_one, dkeys)
    value_grad = contract_first(act_one, dvalues)
    dact_one = (
        contract_last(dqueries, w_query)
        + contract_last(dkeys, w_key)
        + contract_last(dvalues, w_value)
    )
    _, norm_one_back = jax.vjp(rms_scale, frames32, g_attn)
    dframes_norm, attn_gain_grad = norm_one_back(dact_one)
    frames_grad = (dmid + dframes_norm).astype(jnp.bfloat16)
    n_wide = lax.axis_size("wide")
    n_narrow = lax.axis_size("narrow")
    vector_grads = (
        query_bias_grad,
        value_bias_grad,
        out_bias_grad,
        up_bias_grad,
        down_bias_grad,
        attn_gain_grad,
        mlp_gain_grad,
    )
    columns = [
        grad.reshape(n_wide * n_narrow, width_one) for grad, width_one in zip(vector_grads, widths)
    ]
    vector_table = jnp.concatenate(columns, axis=1).reshape(n_wide, n_narrow, -1)
    section = (
        lax.psum_scatter(
            query_grad.astype(jnp.bfloat16), "narrow", scatter_dimension=1, tiled=True
        ).astype(jnp.float32),
        lax.psum_scatter(
            key_grad.astype(jnp.bfloat16), "narrow", scatter_dimension=1, tiled=True
        ).astype(jnp.float32),
        lax.psum_scatter(
            value_grad.astype(jnp.bfloat16), "narrow", scatter_dimension=1, tiled=True
        ).astype(jnp.float32),
        lax.psum_scatter(
            out_grad_w.astype(jnp.bfloat16), "narrow", scatter_dimension=1, tiled=True
        ).astype(jnp.float32),
        lax.psum_scatter(
            up_grad.astype(jnp.bfloat16), "narrow", scatter_dimension=1, tiled=True
        ).astype(jnp.float32),
        lax.psum_scatter(
            down_grad.astype(jnp.bfloat16), "narrow", scatter_dimension=1, tiled=True
        ).astype(jnp.float32),
        lax.psum_scatter(
            vector_table.astype(jnp.bfloat16), "narrow", scatter_dimension=1, tiled=True
        ).astype(jnp.float32),
    )
    final = (
        lax.psum_scatter(
            section[0].astype(jnp.bfloat16), "wide", scatter_dimension=0, tiled=True
        ).astype(jnp.float32),
        lax.psum_scatter(
            section[1].astype(jnp.bfloat16), "wide", scatter_dimension=0, tiled=True
        ).astype(jnp.float32),
        lax.psum_scatter(
            section[2].astype(jnp.bfloat16), "wide", scatter_dimension=0, tiled=True
        ).astype(jnp.float32),
        lax.psum_scatter(
            section[3].astype(jnp.bfloat16), "wide", scatter_dimension=0, tiled=True
        ).astype(jnp.float32),
        lax.psum_scatter(
            section[4].astype(jnp.bfloat16), "wide", scatter_dimension=0, tiled=True
        ).astype(jnp.float32),
        lax.psum_scatter(
            section[5].astype(jnp.bfloat16), "wide", scatter_dimension=0, tiled=True
        ).astype(jnp.float32),
        lax.psum_scatter(
            section[6].astype(jnp.bfloat16), "wide", scatter_dimension=0, tiled=True
        ).astype(jnp.float32),
    )
    flat = final[6].reshape(-1)
    split_grads = []
    offset_one = 0
    for width_one in widths:
        split_grads.append(flat[offset_one : offset_one + width_one])
        offset_one = offset_one + width_one
    return (
        block_out,
        frames_grad,
        final[0],
        final[1],
        final[2],
        final[3],
        final[4],
        final[5],
        split_grads[0],
        split_grads[1],
        split_grads[2],
        split_grads[3],
        split_grads[4],
        split_grads[5],
        split_grads[6],
    )


def plan(mesh):
    nw, nx = mesh.shape["wide"], mesh.shape["narrow"]
    if nx != 2 or nw % 4:
        return None
    return nw // 4, 2, nx


def either(parts, *args):
    d = args[0].shape[1]
    if parts is None or (d // (parts[0] * parts[1])) % 128 or args[3].shape[1] % 256:
        return body(*args)
    return fast_body(*parts, *args)


def solution(mesh):
    return jax.shard_map(
        functools.partial(either, plan(mesh)),
        mesh=mesh,
        in_specs=(
            P(("wide", "narrow"), None),
            P("wide", "narrow"),
            P("wide"),
            P("wide", "narrow"),
            P("wide", "narrow"),
            P("wide", "narrow"),
            P("wide", "narrow"),
            P("wide", "narrow"),
            P("wide", "narrow"),
            P(("wide", "narrow")),
            P(("wide", "narrow")),
            P(("wide", "narrow")),
            P(("wide", "narrow")),
            P(("wide", "narrow")),
            P(("wide", "narrow")),
            P(("wide", "narrow")),
            P(("wide", "narrow"), None),
        ),
        out_specs=(
            P(("wide", "narrow"), None),
            P(("wide", "narrow"), None),
            P("wide", "narrow"),
            P("wide", "narrow"),
            P("wide", "narrow"),
            P("wide", "narrow"),
            P("wide", "narrow"),
            P("wide", "narrow"),
            P(("wide", "narrow")),
            P(("wide", "narrow")),
            P(("wide", "narrow")),
            P(("wide", "narrow")),
            P(("wide", "narrow")),
            P(("wide", "narrow")),
            P(("wide", "narrow")),
        ),
        check_vma=False,
    )
```

```python
import functools
import math

import jax
import jax.numpy as jnp
from jax import lax
from jax.experimental import pallas as pl
from jax.experimental.pallas import tpu as pltpu
from jax.sharding import PartitionSpec as P

HD = 64


EPS = 1e-05

F32 = jnp.float32
BF = jnp.bfloat16


def dot(left, right):
    return jnp.dot(left, right, preferred_element_type=F32)


def dot_last(left, right):
    return lax.dot_general(left, right, (((1,), (1,)), ((), ())), preferred_element_type=F32)


def dot_first(left, right):
    return lax.dot_general(left, right, (((0,), (0,)), ((), ())), preferred_element_type=F32)


def ds(start, size):
    return pl.ds(pl.multiple_of(start, size), size)


def place(sc, p, nz, ny):
    zrel, yrel = p % nz, p // nz
    return lax.rem(sc[0] + nz - zrel, nz) * ny + lax.rem(sc[1] + ny - yrel, ny)


def call(kernel, sc, args, grid, in_specs, out_specs, out_shape, scratch=()):
    spec = pltpu.PrefetchScalarGridSpec(
        num_scalar_prefetch=1,
        grid=grid,
        in_specs=in_specs,
        out_specs=out_specs,
        scratch_shapes=list(scratch),
    )
    return pl.pallas_call(
        kernel,
        grid_spec=spec,
        out_shape=out_shape,
        compiler_params=pltpu.CompilerParams(dimension_semantics=("arbitrary",) * len(grid)),
    )(sc, *args)


def whole(shape):
    return pl.BlockSpec(shape, lambda i, sc: (0,) * len(shape), pipeline_mode=pl.Buffered(1))


def sds(shape, dtype):
    return jax.ShapeDtypeStruct(shape, dtype)


def qkv_kernel(
    sc, own, oth, gain, qb, vb, wa0, wa1, wb0, wb1, q_o, k_o, v_o, a_o, w, tmp, *, nz, ny, blk, grp
):
    i = pl.program_id(0)
    half = pl.num_programs(0) // 2
    n = q_o.shape[1]

    @pl.when(i == 0)
    def _():
        for crel, pair in enumerate(((wa0, wa1), (wb0, wb1))):
            base = lax.rem(sc[2] + crel, 2) * grp
            for p in range(nz * ny):
                rows = ds(place(sc, p, nz, ny) * blk, blk)
                for k in range(3):
                    cols = ds(k * n + base, grp)
                    w[rows, cols] = pair[p // nz][p % nz, :, k * grp : (k + 1) * grp]

    mine = i // half == sc[3]
    f = jnp.where(mine, own[...].astype(F32), oth[...].astype(F32))
    r = lax.rsqrt(jnp.mean(f * f, axis=1, keepdims=True) + EPS)
    tmp[...] = (f * r * gain[...]).astype(BF)
    for p in range(nz * ny):
        a_o[:, p * blk : (p + 1) * blk] = tmp[:, ds(place(sc, p, nz, ny) * blk, blk)]
    act = tmp[...]
    q_o[...] = (dot(act, w[:, :n]) + qb[...]).astype(BF)
    k_o[...] = dot(act, w[:, n : 2 * n]).astype(BF)
    v_o[...] = (dot(act, w[:, 2 * n : 3 * n]) + vb[...]).astype(BF)


def fill_bias(sc, segc, segr, bias, qb):
    total = bias.shape[0]
    for start in range(0, total, qb):
        n = start + qb
        rows = start + lax.broadcasted_iota(jnp.int32, (qb, n), 0)
        cols = lax.broadcasted_iota(jnp.int32, (qb, n), 1)
        ok = (cols <= rows) & (segc[start:n, :] == segr[:, :n])
        ok = ok & ((cols < sc[4]) | (cols == rows))
        bias[start:n, :n] = jnp.where(ok, 0.0, -1000000000.0)


def attn_kernel(sc, segc, segr, q, k, v, c_o, l_o, bias, *, qb):
    p = pl.program_id(0)
    total = q.shape[0]

    @pl.when(p == 0)
    def _():
        fill_bias(sc, segc, segr, bias, qb)
        l_o[...] = jnp.zeros_like(l_o)

    lane = lax.broadcasted_iota(jnp.int32, (qb, 128), 1)
    for start in range(0, total, qb):
        n = start + qb
        outs = []
        lse = l_o[start:n, :]
        for h in range(2):
            lo, hi = h * HD, (h + 1) * HD
            qh = q[start:n, lo:hi] * jnp.asarray(1.0 / math.sqrt(HD), BF)
            s = dot_last(qh, k[:n, lo:hi]) + bias[start:n, :n]
            top = jnp.max(s, axis=1, keepdims=True)
            e = jnp.exp(s - top)
            t = jnp.sum(e, axis=1, keepdims=True)
            pr = (e * (1.0 / t)).astype(BF)
            outs.append(dot(pr, v[:n, lo:hi]))
            lse = jnp.where(lane == 2 * p + h, top + jnp.log(t), lse)
        l_o[start:n, :] = lse
        c_o[start:n, :] = jnp.concatenate(outs, axis=1).astype(BF)


def attn_back_kernel(
    sc, segc, segr, q, k, v, d, l, dq_o, dk_o, dv_o, qs_o, vs_o, bias, dks, dvs, *, qb
):
    p = pl.program_id(0)
    total = q.shape[0]

    @pl.when(p == 0)
    def _():
        fill_bias(sc, segc, segr, bias, qb)

    lane = lax.broadcasted_iota(jnp.int32, (qb, 128), 1)
    scale = jnp.asarray(1.0 / math.sqrt(HD), BF)
    for start in range(total - qb, -1, -qb):
        n = start + qb
        dqs, dkk, dvv = [], [], []
        for h in range(2):
            lo, hi = h * HD, (h + 1) * HD
            qh = q[start:n, lo:hi] * scale
            kh, vh, dh = k[:n, lo:hi], v[:n, lo:hi], d[start:n, lo:hi]
            lse = jnp.sum(jnp.where(lane == 2 * p + h, l[start:n, :], 0.0), axis=1, keepdims=True)
            pr = jnp.exp(dot_last(qh, kh) + bias[start:n, :n] - lse)
            dp = dot_last(dh, vh)
            inner = jnp.sum(pr * dp, axis=1, keepdims=True)
            dsc = (pr * (dp - inner)).astype(BF)
            dqs.append(dot(dsc, kh) * (1.0 / math.sqrt(HD)))
            dkk.append(dot_first(dsc, qh))
            dvv.append(dot_first(pr.astype(BF), dh))
        dq_o[start:n, :] = jnp.concatenate(dqs, axis=1).astype(BF)
        dkk, dvv = jnp.concatenate(dkk, axis=1), jnp.concatenate(dvv, axis=1)
        if n == total:
            dks[...] = dkk
            dvs[...] = dvv
        else:
            dks[:n, :] += dkk
            dvs[:n, :] += dvv
    dk_o[...] = dks[...].astype(BF)
    dvb = dvs[...].astype(BF)
    dv_o[...] = dvb
    qs_o[...] = jnp.sum(dq_o[...].astype(F32), axis=0, keepdims=True)
    vs_o[...] = jnp.sum(dvb.astype(F32), axis=0, keepdims=True)


def out_kernel(
    sc, cown, coth, fr, ob, gain, w00, w01, w10, w11, cx_o, mid_o, a_o, w, tmp,
    *, nz, ny, nx, blk, grp,
):
    hw = cown.shape[1]
    x = sc[3]

    @pl.when(pl.program_id(0) == 0)
    def _():
        for xrel, pair in enumerate(((w00, w01), (w10, w11))):
            for crel, part in enumerate(pair):
                base = lax.rem(x + xrel, nx) * hw + lax.rem(sc[2] + crel, 2) * grp
                for p in range(nz * ny):
                    got = part[p // nz, p % nz]
                    zy = place(sc, p, nz, ny)
                    for side in range(2):
                        rows = ds(zy * blk + side * (blk // 2), blk // 2)
                        w[rows, ds(base, grp)] = got[:, side * grp : (side + 1) * grp]

    cx_o[:, ds(x * hw, hw)] = cown[...]
    cx_o[:, ds((1 - x) * hw, hw)] = coth[...]
    mid = fr[...].astype(F32) + dot(cx_o[...], w[...]) + ob[...]
    mid_o[...] = mid
    r = lax.rsqrt(jnp.mean(mid * mid, axis=1, keepdims=True) + EPS)
    tmp[...] = (mid * r * gain[...]).astype(BF)
    for p in range(nz * ny):
        a_o[:, p * blk : (p + 1) * blk] = tmp[:, ds(place(sc, p, nz, ny) * blk, blk)]


def mlp_kernel(
    sc, a0, a1, d0, d1, ub, up0, up1, dn0, dn1,
    bo_o, bs_o, da_o, ds_o, uo_o, us_o, do_o, dos_o, ug_o,
    act, act_t, dr, bacc, dacc,
):
    t = pl.program_id(0)
    m = a0.shape[0]
    hw = dn0.shape[3]
    x = sc[3]

    @pl.when(t == 0)
    def _():
        for row, (a, d) in enumerate(((a0, d0), (a1, d1))):
            act[row * m : (row + 1) * m, :] = a[...]
            act_t[:, row * m : (row + 1) * m] = a[...].T
            dr[row * m : (row + 1) * m, :hw] = d[:, ds(x * hw, hw)]
            dr[row * m : (row + 1) * m, hw:] = d[:, ds((1 - x) * hw, hw)]
        bacc[...] = jnp.zeros_like(bacc)
        dacc[...] = jnp.zeros_like(dacc)

    nz, ff = up0.shape[0], up0.shape[3]
    k = nz * up0.shape[2]
    u0 = up0[...].reshape(k, ff)
    u1 = up1[...].reshape(k, ff)
    w0 = dn0[...].reshape(ff, hw)
    w1 = dn1[...].reshape(ff, hw)
    pre = dot(act[:, :k], u0) + dot(act[:, k:], u1) + ub[...].reshape(1, ff)
    dh = dot_last(dr[:, :hw], w0) + dot_last(dr[:, hw:], w1)
    sq = pre * pre
    th = jnp.tanh(pre * (0.7978845608 + (0.7978845608 * 0.044715) * sq))
    hp = 0.5 * (1.0 + th)
    hid = (pre * hp).astype(BF)
    slope = hp + (0.5 * pre) * (1.0 - th * th) * (
        0.7978845608 + (3.0 * 0.7978845608 * 0.044715) * sq
    )
    dpre = (dh * slope).astype(BF)
    bacc[:, :hw] += dot(hid, w0)
    bacc[:, hw:] += dot(hid, w1)
    dacc[:, :k] += dot_last(dpre, u0)
    dacc[:, k:] += dot_last(dpre, u1)
    uo_o[...] = dot(act_t[:k, :], dpre).astype(BF).reshape(1, k, ff)
    us_o[...] = dot(act_t[k:, :], dpre).astype(BF).reshape(1, k, ff)
    hid_t = hid.T
    do_o[...] = dot(hid_t, dr[:, :hw]).astype(BF).reshape(1, ff, hw)
    dos_o[...] = dot(hid_t, dr[:, hw:]).astype(BF).reshape(1, ff, hw)
    ug_o[...] = jnp.sum(dpre.astype(F32), axis=0, keepdims=True).reshape(1, 1, ff)

    @pl.when(t == pl.num_programs(0) - 1)
    def _():
        bo_o[...] = bacc[:m, :]
        bs_o[...] = bacc[m:, :].astype(BF)
        da_o[...] = dacc[:m, :]
        ds_o[...] = dacc[m:, :].astype(BF)


def mid_kernel(
    sc, da0, da1, dr0, dr1, bo0, bo1, br0, br1, mid, do, gain, db, cx, w,
    blk_o, dmid_o, dco_o, dcs_o, wo_o, ws_o, vec_o,
    tmp, dcx, acc, *, nz, ny, nx, blk, grp,
):
    i = pl.program_id(0)
    x = sc[3]
    hw = tmp.shape[1] // nx

    @pl.when(i == 0)
    def _():
        vec_o[...] = jnp.zeros_like(vec_o)
        acc[...] = jnp.zeros_like(acc)

    def total(parts, lo, hi):
        got = parts[0][:, lo:hi].astype(F32)
        for part in parts[1:]:
            got = got + part[:, lo:hi].astype(F32)
        return got

    mv = mid[...]
    for xrel in range(nx):
        part = total((bo0, bo1, br0, br1), xrel * hw, (xrel + 1) * hw)
        tmp[:, ds(lax.rem(x + xrel, nx) * hw, hw)] = part
    blk_o[...] = (mv + tmp[...] + db[...]).astype(BF)
    for p in range(nz * ny):
        part = total((da0, da1, dr0, dr1), p * blk, (p + 1) * blk)
        tmp[:, ds(place(sc, p, nz, ny) * blk, blk)] = part
    dact = tmp[...]
    r = lax.rsqrt(jnp.mean(mv * mv, axis=1, keepdims=True) + EPS)
    n = mv * r
    dn = dact * gain[...]
    dout = do[...].astype(F32)
    dmid = dout + r * (dn - n * jnp.mean(dn * n, axis=1, keepdims=True))
    dmid_o[...] = dmid
    dattn = dmid.astype(BF)
    vec_o[0:1, :] += jnp.sum(dact * n, axis=0, keepdims=True)
    vec_o[1:2, :] += jnp.sum(dattn.astype(F32), axis=0, keepdims=True)
    vec_o[2:3, :] += jnp.sum(dout, axis=0, keepdims=True)
    dcx[...] = dot_last(dattn, w[...]).astype(BF)
    heads = dco_o.shape[1]
    dco_o[...] = dcx[:, ds(x * heads, heads)]
    dcs_o[...] = dcx[:, ds((1 - x) * heads, heads)]
    acc[...] += dot(cx[...].T, dattn)

    @pl.when(i == pl.num_programs(0) - 1)
    def _():
        for xrel in range(nx):
            for crel, out in enumerate((wo_o, ws_o)):
                base = lax.rem(x + xrel, nx) * heads + lax.rem(sc[2] + crel, 2) * grp
                for p in range(nz * ny):
                    rows = ds(place(sc, p, nz, ny) * blk, blk)
                    out[xrel, p] = acc[rows, ds(base, grp)].astype(BF)


def gain_part(w, got, cols, hd, grp):
    total = None
    for k in range(3):
        prod = w[:, ds(k * hd + cols, grp)].astype(F32) * got[:, k * grp : (k + 1) * grp]
        for lo in range(0, grp, 128):
            part = prod[:, lo : lo + 128]
            total = part if total is None else total + part
    return jnp.sum(total.T, axis=0, keepdims=True)


def give_kernel(sc, ar, dq, dk, dv, w, o, g_o, *, hd, grp):
    cat = jnp.concatenate([dq[...], dk[...], dv[...]], axis=1)
    got = dot(ar[...].T, cat)
    o[...] = got.astype(BF).reshape(o.shape)
    g_o[...] = gain_part(w, got, (1 - sc[2]) * grp, hd, grp).reshape(g_o.shape)


def keep_kernel(
    sc, ar, dq, dk, dv, w, rec, gg, gain, qs, vs, vm, gu0, gu1, o, *, nz, ny, nx, hd, grp, blk
):
    p = pl.program_id(0)
    zy = place(sc, p, nz, ny)
    cat = jnp.concatenate([dq[...], dk[...], dv[...]], axis=1)
    got = dot(ar[...].T, cat)
    o[0, :blk, :] = (got + rec[0].astype(F32)).astype(BF)
    gsum = (gain_part(w, got, sc[2] * grp, hd, grp) + gg[0]) / gain[:, ds(zy * blk, blk)]
    nbx = nz * ny // nx
    here = zy // nbx == sc[3]
    local = ds(lax.rem(zy, nbx) * blk, blk)
    lanes = ds(zy * blk, blk)
    parts = (
        jnp.where(here, qs[:, local], 0.0),
        jnp.where(here, vs[:, local], 0.0),
        vm[1:2, lanes],
        vm[2:3, lanes],
        gsum,
        vm[0:1, lanes],
    )
    o[0, blk:, :] = jnp.zeros((o.shape[1] - blk, o.shape[2]), BF)
    for k, part in enumerate(parts):
        o[0, blk : blk + 1, k * blk : (k + 1) * blk] = part.astype(BF)
    ffb = gu0.shape[2]
    piece = jnp.where(lax.rem(p, 2) == 0, gu0[0], gu1[0])
    o[0, blk + 1 : blk + 2, ds(sc[2] * ffb, ffb)] = piece.astype(BF)


def dact_kernel(sc, dq, dk, dv, w, da_o, ds_o):
    i = pl.program_id(0)
    half = pl.num_programs(0) // 2
    cat = jnp.concatenate([dq[...], dk[...], dv[...]], axis=1)
    dact = dot_last(cat, w[...])

    @pl.when(i >= half)
    def _():
        da_o[...] = dact

    @pl.when(i < half)
    def _():
        ds_o[...] = dact.astype(BF)


def last_kernel(sc, da, dr, dmid, fr, gain, o):
    f = fr[...].astype(F32)
    r = lax.rsqrt(jnp.mean(f * f, axis=1, keepdims=True) + EPS)
    n = f * r
    dn = (da[...] + dr[...].astype(F32)) * gain[...]
    o[...] = (dmid[...] + r * (dn - n * jnp.mean(dn * n, axis=1, keepdims=True))).astype(BF)


def add_low(*parts):
    total = parts[0].astype(F32)
    for part in parts[1:]:
        total = total + part.astype(F32)
    return total


def fast_body(nz, ny, nx, *args):
    (
        frames, segment_ids, row_length, query_proj, key_proj, value_proj, out_proj, up_proj,
        down_proj, query_bias, value_bias, out_bias, up_bias, down_bias, attn_gain, mlp_gain,
        out_grad,
    ) = args
    nw = nz * ny * 2
    nb = nz * ny
    w = lax.axis_index("wide")
    x = lax.axis_index("narrow")
    c = lax.rem(w, 2)
    y = lax.rem(w // 2, ny)
    z = w // (2 * ny)
    m, d = frames.shape
    rows = m * nx
    blk = d // nb
    grp = query_proj.shape[1] // 2
    wr = query_proj.shape[0]
    ffb = down_proj.shape[0]
    ffx = up_proj.shape[1] // 2
    nj = ffx // ffb
    hw = d // nx

    def send_w(a, dz=0, dy=0, dc=0):
        perm = []
        for i in range(nw):
            zi, yi, ci = i // (2 * ny), (i // 2) % ny, i % 2
            perm.append((i, (((zi + dz) % nz) * ny + (yi + dy) % ny) * 2 + (ci + dc) % 2))
        return lax.ppermute(a, "wide", perm)

    def send_x(a, k=1):
        return lax.ppermute(a, "narrow", [(i, (i + k) % nx) for i in range(nx)])

    def send_xc(a):
        perm = []
        for i in range(nw):
            for j in range(nx):
                perm.append((i * nx + j, (i ^ 1) * nx + (j + 1) % nx))
        return lax.ppermute(a, ("wide", "narrow"), perm)

    def pick(flag, a, b):
        return jnp.where(flag == 0, a, b)

    def in_order(flag, own, oth, axis=0):
        return pick(
            flag, jnp.concatenate([own, oth], axis=axis), jnp.concatenate([oth, own], axis=axis)
        )

    def tie(values, *deps):
        flat = lax.optimization_barrier((tuple(values), deps))
        return flat[0]

    vectors = (query_bias, value_bias, out_bias, up_bias, down_bias, attn_gain, mlp_gain)
    widths = [piece.shape[0] for piece in vectors]
    nv = sum(widths)
    packed = jnp.zeros((nv,), BF)
    offset = 0
    for piece, width in zip(vectors, widths):
        packed = packed + jnp.pad(piece, (offset, nv - offset - width))
        offset = offset + width
    segs = segment_ids[0]
    tail = jnp.pad(packed, (0, m)) + jnp.pad(segs.astype(BF), (nv, 0))
    vec_x = send_x(tail)
    vec_xc = send_xc(packed)
    vec_c = send_w(packed, dc=1)

    def halves_of(a):
        return a[:, :grp], a[:, grp:]

    def trade(sides):
        keep, give = pick(c, sides[0], sides[1]), pick(c, sides[1], sides[0])
        return in_order(c, keep, send_w(give, dc=1))

    qs, ks, vs, os = [halves_of(a) for a in (query_proj, key_proj, value_proj, out_proj)]
    pair = trade([jnp.concatenate([qs[e], ks[e], vs[e]], axis=1) for e in range(2)])
    up4 = up_proj.reshape(wr, nj, 2, ffb)
    uo_pair = trade(
        [jnp.concatenate([up4[:, :, e].reshape(wr, ffx), os[e]], axis=1) for e in range(2)]
    )

    def along_z(a):
        return [a] + [send_w(a, dz=k) for k in range(1, nz)]

    in_z = along_z(pair)
    own_vec = in_order(x, packed[None], vec_x[None, :nv])
    oth_vec = in_order(x, vec_c[None], vec_xc[None])
    vec4 = in_order(c, own_vec, oth_vec).reshape(-1)
    tail_rows = 16
    count = vec4.shape[0]
    vec_block = jnp.pad(vec4, (0, tail_rows * 3 * grp - count)).reshape(tail_rows, 3 * grp)
    vec_z = along_z(vec_block)
    in_y = jnp.stack([jnp.concatenate([a, b]) for a, b in zip(in_z, vec_z)])
    wa = [in_y, send_w(in_y, dy=1)]
    wb = [send_w(a, dc=1) for a in wa]

    (frames_go,) = tie((frames,), vec_x, vec_xc)
    frames_oth = send_x(frames_go)
    (dout_go,) = tie((out_grad,), vec_xc)
    dout_par = send_w(dout_go, dc=1)
    (uo_go,) = tie((uo_pair,), frames_oth)
    uo_x = jnp.stack([uo_pair, send_x(uo_go)])

    out_pair = uo_pair[:, ffx:]
    out_block = jnp.concatenate([out_pair[:blk // 2], out_pair[blk // 2 :]], axis=1)
    (dn,) = tie((jnp.concatenate([down_proj, out_block]),), *in_z[1:])
    dn_z = along_z(dn)
    dn_y = jnp.stack(dn_z)
    (dn_go,) = tie((dn_y,), wa[1])
    dn_y = [dn_y, send_w(dn_go, dy=1)]
    ow = jnp.stack([a[:, ffb:] for a in dn_y])
    out_w = [ow, send_x(ow)]
    out_wc = [send_w(a, dc=1) for a in out_w]
    hz = nz // 2
    dns = [jnp.stack([a[e::2, :ffb] for a in dn_y]) for e in range(2)]

    ups = [uo_x[:, :, e * (ffx // 2) : (e + 1) * (ffx // 2)] for e in range(2)]
    ups = [pick(z % 2, ups[0], ups[1]), pick(z % 2, ups[1], ups[0])]

    def up_part(e, *deps):
        use = tie((ups[e], ups[1 - e]), *deps)
        got = [use[0]] + [send_w(use[k % 2], dz=k) for k in range(1, nz)]
        return jnp.stack(got), got[-1]

    up_z0, z0_done = up_part(0, *dn_z[1:])
    up_z1, _ = up_part(1, z0_done)
    up_y = [[a, send_w(a, dy=1)] for a in (up_z0, up_z1)]

    table = jnp.stack([a[:, 2 * wr :].reshape(nz, -1)[:, :count] for a in wa]).reshape(nb, count)
    here = jnp.arange(nb)
    back = lax.rem(y + ny - here % ny, ny) * nz + lax.rem(z + nz - here // ny, nz)
    table = dot((back[:, None] == here[None, :]).astype(BF), table).reshape(nw * nx, nv)
    full_vec = []
    offset = 0
    for width in widths:
        full_vec.append(table[:, offset : offset + width].reshape(1, -1))
        offset = offset + width
    b_query, b_value, b_out, b_up, b_down, g_attn, g_mlp = full_vec
    qb = lax.dynamic_slice(b_query, (0, x * 2 * grp), (1, 2 * grp))
    vb = lax.dynamic_slice(b_value, (0, x * 2 * grp), (1, 2 * grp))
    ub = lax.dynamic_index_in_dim(b_up.reshape(nb, 2, ffb), c, axis=1)

    sc_at = jnp.arange(5, dtype=jnp.int32)
    sc = jnp.where(sc_at == 0, z, jnp.where(sc_at == 1, y, jnp.where(sc_at == 2, c, x)))
    sc = jnp.where(sc_at == 4, row_length[0], sc).astype(jnp.int32)

    seg_row = in_order(x, segs, vec_x[nv:].astype(jnp.int32))
    segc, segr = seg_row.reshape(rows, 1), seg_row.reshape(1, rows)

    rb = min(256, m)
    steps = rows // rb
    per = m // rb
    hd = 2 * grp
    wspec = whole((d, 3 * hd))
    wpart = whole((nz, 2 * wr, 3 * grp))
    dims = dict(nz=nz, ny=ny, blk=blk)
    row_own = pl.BlockSpec((rb, d), lambda i, sc: (i % per, 0))
    wide_row = pl.BlockSpec((rb, d), lambda i, sc: (i, 0))
    heads_row = pl.BlockSpec((rb, hd), lambda i, sc: (i, 0))
    q, k, v, act_one, w_in = call(
        functools.partial(qkv_kernel, grp=grp, **dims),
        sc,
        (frames, frames_oth, g_attn, qb, vb, *wa, *wb),
        (steps,),
        [row_own, row_own, whole((1, d)), whole((1, hd)), whole((1, hd))] + [wpart] * 4,
        [heads_row, heads_row, heads_row, wide_row, wspec],
        [sds((rows, hd), BF)] * 3 + [sds((rows, d), BF), sds((d, 3 * hd), BF)],
        [pltpu.VMEM((rb, d), BF)],
    )

    pairs = hd // 128
    qblk = min(256, rows)
    pair_spec = pl.BlockSpec((rows, 128), lambda i, sc: (0, i))
    ctx, lse = call(
        functools.partial(attn_kernel, qb=qblk),
        sc,
        (segc, segr, q, k, v),
        (pairs,),
        [whole((rows, 1)), whole((1, rows)), pair_spec, pair_spec, pair_spec],
        [pair_spec, whole((rows, 128))],
        [sds((rows, hd), BF), sds((rows, 128), F32)],
        [pltpu.VMEM((rows, rows), F32)],
    )
    (ctx,) = tie((ctx,), z0_done)
    ctx_own = lax.dynamic_slice(ctx, (x * m, 0), (m, hd))
    ctx_oth = send_x(lax.dynamic_slice(ctx, ((1 - x) * m, 0), (m, hd)))

    ospec = whole((d, d))
    fsteps = m // rb
    owpart = whole((ny, nz, blk // 2, hd))
    ctx_full, mid, act_own, w_out = call(
        functools.partial(out_kernel, nx=nx, grp=grp, **dims),
        sc,
        (ctx_own, ctx_oth, frames, b_out, g_mlp, out_w[0], out_wc[0], out_w[1], out_wc[1]),
        (fsteps,),
        [heads_row, heads_row, wide_row, whole((1, d)), whole((1, d))] + [owpart] * 4,
        [wide_row, wide_row, wide_row, ospec],
        [sds((m, d), BF), sds((m, d), F32), sds((m, d), BF), sds((d, d), BF)],
        [pltpu.VMEM((rb, d), BF)],
    )
    act_par = send_w(act_own, dc=1)
    dn0_x = send_x(dns[0])
    (dn1_go,) = tie((dns[1],), ctx_oth, dn0_x)
    dn_x = [[dns[0], dn0_x], [dns[1], send_x(dn1_go)]]

    kk = nz * blk

    def feed_forward(odd):
        def at(t, sc):
            zy = place(sc, (t // hz) * nz + odd + 2 * (t % hz), nz, ny)
            return zy, lax.rem(sc[3] + nx - zy // nj, nx), lax.rem(zy, nj)

        def up_in(t, sc):
            _, xrel, j = at(t, sc)
            return (0, xrel, 0, j % ny)

        def up_out(t, sc):
            _, xrel, j = at(t, sc)
            return (xrel, 0, j % ny)

        upspec = pl.BlockSpec((nz, 1, blk, ffb), up_in)
        dnspec = pl.BlockSpec((1, 1, ffb, hw), lambda t, sc: (t // hz, t % hz, 0, 0))
        bspec = pl.BlockSpec((1, 1, ffb), lambda t, sc: (at(t, sc)[0], 0, 0))
        tspec = pl.BlockSpec((1, 1, ffb), lambda t, sc: (t, 0, 0))
        return call(
            mlp_kernel,
            sc,
            (act_own, act_par, out_grad, dout_par, ub, *up_y[odd], *dn_x[odd]),
            (ny * hz,),
            [whole((m, d))] * 4 + [bspec, upspec, upspec, dnspec, dnspec],
            [whole((m, d))] * 4
            + [pl.BlockSpec((1, kk, ffb), up_out)] * 2
            + [pl.BlockSpec((1, ffb, hw), lambda t, sc: (t, 0, 0))] * 2
            + [tspec],
            [sds((m, d), F32), sds((m, d), BF), sds((m, d), F32), sds((m, d), BF)]
            + [sds((nx, kk, ny * ffb), BF)] * 2
            + [sds((ny * hz, ffb, hw), BF)] * 2
            + [sds((ny * hz, 1, ffb), F32)],
            [
                pltpu.VMEM((2 * m, d), BF),
                pltpu.VMEM((d, 2 * m), BF),
                pltpu.VMEM((2 * m, d), BF),
                pltpu.VMEM((2 * m, d), F32),
                pltpu.VMEM((2 * m, d), F32),
            ],
        )

    halves = []
    for odd in range(2):
        got = feed_forward(odd)
        if odd:
            got = tie(got, halves[0]["gd_got"], halves[0]["gu_raw"])
        bo, bo_give, da, da_give, gu, gu_give, gd, gd_give, g_up = got
        gu_raw = send_w(gu_give, dy=-1)
        halves.append(
            dict(
                bo=bo,
                da=da,
                gu=gu.reshape(nx, nz, blk, ny * ffb),
                gd=gd,
                g_up=g_up,
                bo_got=send_w(bo_give, dc=1),
                da_got=send_w(da_give, dc=1),
                gd_got=send_x(gd_give),
                gu_raw=gu_raw,
                gu_got=gu_raw.reshape(nx, nz, blk, ny * ffb),
            )
        )

    def first_sums(h):
        gd = add_low(h["gd"], h["gd_got"]).astype(BF)
        gu = [add_low(h["gu"][:, e], h["gu_got"][:, e]).astype(BF) for e in range(nz)]
        return gd, gu

    gd_0, gu_0 = first_sums(halves[0])

    mid_args = (
        halves[0]["da"], halves[1]["da"], halves[0]["da_got"], halves[1]["da_got"],
        halves[0]["bo"], halves[1]["bo"], halves[0]["bo_got"], halves[1]["bo_got"],
    )
    block_out, dmid, dctx_own, dctx_give, wo, wo_give, vec_mid = call(
        functools.partial(mid_kernel, nx=nx, grp=grp, **dims),
        sc,
        (*mid_args, mid, out_grad, g_mlp, b_down, ctx_full, w_out),
        (fsteps,),
        [wide_row] * 10 + [whole((1, d)), whole((1, d)), wide_row, ospec],
        [wide_row, wide_row, heads_row, heads_row]
        + [whole((nx, nb, blk, grp))] * 2
        + [whole((8, d))],
        [sds((m, d), BF), sds((m, d), F32), sds((m, hd), BF), sds((m, hd), BF)]
        + [sds((nx, nb, blk, grp), BF)] * 2
        + [sds((8, d), F32)],
        [pltpu.VMEM((rb, d), F32), pltpu.VMEM((rb, d), BF), pltpu.VMEM((d, d), F32)],
    )
    dctx = in_order(x, dctx_own, send_x(dctx_give))
    wo = add_low(wo, send_w(wo_give, dc=1)).astype(BF)
    wo_got = send_x(wo[1])

    gd_1, gu_1 = first_sums(halves[1])
    (dctx,) = tie((dctx,), gd_1, gu_1)
    dq, dk, dv, qsum, vsum = call(
        functools.partial(attn_back_kernel, qb=qblk),
        sc,
        (segc, segr, q, k, v, dctx, lse),
        (pairs,),
        [whole((rows, 1)), whole((1, rows)), pair_spec, pair_spec, pair_spec, pair_spec]
        + [whole((rows, 128))],
        [pair_spec] * 3 + [pl.BlockSpec((1, 128), lambda i, sc: (0, i))] * 2,
        [sds((rows, hd), BF)] * 3 + [sds((1, hd), F32)] * 2,
        [
            pltpu.VMEM((rows, rows), F32),
            pltpu.VMEM((rows, 128), F32),
            pltpu.VMEM((rows, 128), F32),
        ],
    )

    wo = add_low(wo[0], wo_got).astype(BF)
    wo = jnp.concatenate([wo[:, : blk // 2], wo[:, blk // 2 :]], axis=2)
    gd_y = []
    for yrel in range(ny):
        parts = [(gd_0, gd_1)[e % 2][yrel * hz + e // 2] for e in range(nz)]
        gd_y.append(jnp.concatenate([jnp.stack(parts), wo[yrel * nz : (yrel + 1) * nz]], axis=1))
    gd_2 = add_low(gd_y[0], send_w(gd_y[1], dy=-1)).astype(BF)
    gu_2 = [in_order(z % 2, a, b, axis=2) for a, b in zip(gu_0, gu_1)]
    gu_z = [send_w(gu_2[e], dz=-e) for e in range(1, nz)]
    dq, dk, dv = tie((dq, dk, dv), gd_2)

    def col_rel(e):
        return pl.BlockSpec((rows, grp), lambda p, sc: (0, lax.rem(sc[2] + e, 2)))

    def block_of(shape):
        return pl.BlockSpec(shape, lambda p, sc: (p,) + (0,) * (len(shape) - 1))

    ar_spec = pl.BlockSpec((rows, blk), lambda p, sc: (0, p))
    wrow = pl.BlockSpec((blk, 3 * hd), lambda p, sc: (place(sc, p, nz, ny), 0))
    wg_give, gain_give = call(
        functools.partial(give_kernel, hd=hd, grp=grp),
        sc,
        (act_one, dq, dk, dv, w_in),
        (nb,),
        [ar_spec, col_rel(1), col_rel(1), col_rel(1), wrow],
        [block_of((1, blk, 3 * grp)), block_of((1, 1, blk))],
        [sds((nb, blk, 3 * grp), BF), sds((nb, 1, blk), F32)],
    )
    wg_got = send_w(wg_give, dc=1)
    gu_spec = pl.BlockSpec((1, 1, ffb), lambda p, sc: ((p // nz) * hz + (p % nz) // 2, 0, 0))
    wg = call(
        functools.partial(keep_kernel, nx=nx, hd=hd, grp=grp, **dims),
        sc,
        (
            act_one, dq, dk, dv, w_in, wg_got, gain_give, g_attn, qsum, vsum, vec_mid,
            halves[0]["g_up"], halves[1]["g_up"],
        ),
        (nb,),
        [ar_spec, col_rel(0), col_rel(0), col_rel(0), wrow]
        + [block_of((1, blk, 3 * grp)), block_of((1, 1, blk)), whole((1, d))]
        + [whole((1, hd)), whole((1, hd)), whole((8, d)), gu_spec, gu_spec],
        block_of((1, blk + tail_rows, 3 * grp)),
        sds((nb, blk + tail_rows, 3 * grp), BF),
    )
    gq_got = send_w(wg[nz:], dy=-1)

    def abs_rows(i, sc):
        return (lax.rem(i + (1 - sc[3]) * per, 2 * per), 0)

    order_row = pl.BlockSpec((rb, hd), abs_rows)
    late = pl.BlockSpec((rb, d), lambda i, sc: (jnp.maximum(i - per, 0), 0))
    early = pl.BlockSpec((rb, d), lambda i, sc: (jnp.minimum(i, per - 1), 0))
    (dq,) = tie((dq,), wg)
    dact, dact_give = call(
        dact_kernel,
        sc,
        (dq, dk, dv, w_in),
        (steps,),
        [order_row] * 3 + [wspec],
        [late, early],
        [sds((m, d), F32), sds((m, d), BF)],
    )
    dact_got = send_x(dact_give)

    gd_3 = add_low(gd_2[0], *[send_w(gd_2[e], dz=-e) for e in range(1, nz)])
    down_grad = gd_3[:ffb]
    gu_3 = add_low(gu_2[0], *gu_z).astype(BF)
    gu_4 = add_low(gu_3[0], send_x(gu_3[1]))
    go_4 = jnp.concatenate([gd_3[ffb:, :grp], gd_3[ffb:, grp:]], axis=0)

    gq = add_low(wg[:nz], gq_got).astype(BF)
    (dact_got,) = tie((dact_got,), gq)
    gq = add_low(gq[0], *[send_w(gq[e], dz=-e) for e in range(1, nz)])

    last = jnp.concatenate([gu_4, gq[:blk], go_4], axis=1)
    mine = lax.dynamic_slice(last, (c * wr, 0), (wr, last.shape[1]))
    theirs = send_w(
        lax.dynamic_slice(last, ((1 - c) * wr, 0), (wr, last.shape[1])).astype(BF), dc=1
    ).astype(F32)
    sides = (pick(c, mine, theirs), pick(c, theirs, mine))
    up_grad = jnp.stack([s[:, :ffx].reshape(wr, nj, ffb) for s in sides], axis=2)
    up_grad = up_grad.reshape(wr, 2 * ffx)
    weights = []
    for at in range(4):
        lo = ffx + at * grp
        weights.append(jnp.concatenate([s[:, lo : lo + grp] for s in sides], axis=1))

    small = gq[blk : blk + 2]
    small = small + send_w(small, dc=1)
    small = small + send_x(small)
    who = c * nx + x
    vec6 = small[0].reshape(6, blk)
    vec6 = lax.dynamic_slice(vec6, (0, who * (blk // (2 * nx))), (6, blk // (2 * nx)))
    per_ff = 2 * ffb // (2 * nx)
    vec_up = lax.dynamic_slice(small[1], (who * per_ff,), (per_ff,))
    vec_out = (vec6[0], vec6[1], vec6[2], vec_up, vec6[3], vec6[4], vec6[5])

    frames_grad = call(
        last_kernel,
        sc,
        (dact, dact_got, dmid, frames, g_attn),
        (fsteps,),
        [wide_row] * 4 + [whole((1, d))],
        wide_row,
        sds((m, d), BF),
    )
    return (block_out, frames_grad, *weights, up_grad, down_grad, *vec_out)


def product(left, right):
    return jnp.dot(left, right, preferred_element_type=jnp.float32)


def contract_first(left, right):
    return lax.dot_general(
        left, right, (((0,), (0,)), ((), ())), preferred_element_type=jnp.float32
    )


def contract_last(left, right):
    return lax.dot_general(
        left, right, (((1,), (1,)), ((), ())), preferred_element_type=jnp.float32
    )


def rms_scale(values, gain):
    return values * lax.rsqrt(jnp.mean(values * values, axis=-1, keepdims=True) + EPS) * gain


def gather_params(shards):
    inner = (
        lax.all_gather(shards[0], "narrow", axis=1, tiled=True),
        lax.all_gather(shards[1], "narrow", axis=1, tiled=True),
        lax.all_gather(shards[2], "narrow", axis=1, tiled=True),
        lax.all_gather(shards[3], "narrow", axis=1, tiled=True),
        lax.all_gather(shards[4], "narrow", axis=1, tiled=True),
        lax.all_gather(shards[5], "narrow", axis=1, tiled=True),
        lax.all_gather(shards[6], "narrow", axis=1, tiled=True),
    )
    return (
        lax.all_gather(inner[0], "wide", axis=0, tiled=True),
        lax.all_gather(inner[1], "wide", axis=0, tiled=True),
        lax.all_gather(inner[2], "wide", axis=0, tiled=True),
        lax.all_gather(inner[3], "wide", axis=0, tiled=True),
        lax.all_gather(inner[4], "wide", axis=0, tiled=True),
        lax.all_gather(inner[5], "wide", axis=0, tiled=True),
        lax.all_gather(inner[6], "wide", axis=0, tiled=True),
    )


def gather_again(shards):
    inner = (
        lax.all_gather(shards[0], "narrow", axis=1, tiled=True),
        lax.all_gather(shards[1], "narrow", axis=1, tiled=True),
        lax.all_gather(shards[2], "narrow", axis=1, tiled=True),
        lax.all_gather(shards[3], "narrow", axis=1, tiled=True),
        lax.all_gather(shards[4], "narrow", axis=1, tiled=True),
        lax.all_gather(shards[5], "narrow", axis=1, tiled=True),
        lax.all_gather(shards[6], "narrow", axis=1, tiled=True),
    )
    return (
        lax.all_gather(inner[0], "wide", axis=0, tiled=True),
        lax.all_gather(inner[1], "wide", axis=0, tiled=True),
        lax.all_gather(inner[2], "wide", axis=0, tiled=True),
        lax.all_gather(inner[3], "wide", axis=0, tiled=True),
        lax.all_gather(inner[4], "wide", axis=0, tiled=True),
        lax.all_gather(inner[5], "wide", axis=0, tiled=True),
        lax.all_gather(inner[6], "wide", axis=0, tiled=True),
    )


def unpack_vectors(packed, widths):
    table = packed.reshape(-1, packed.shape[-1])
    pieces = []
    offset = 0
    for width in widths:
        pieces.append(table[:, offset : offset + width].reshape(-1).astype(jnp.float32))
        offset = offset + width
    return pieces


def build_mask(own_segments, row_segments, limit, offset, start, count):
    total = row_segments.shape[0]
    rows = offset + start + lax.broadcasted_iota(jnp.int32, (count, total), 0)
    cols = lax.broadcasted_iota(jnp.int32, (count, total), 1)
    same = own_segments[:, None] == row_segments[None, :]
    return (cols <= rows) & same & ((cols < limit) | (cols == rows))


def attend(query_part, key_part, value_part, allowed):
    scale = 1.0 / math.sqrt(HD)
    q3 = query_part.reshape(query_part.shape[0], -1, HD)
    k3 = key_part.reshape(key_part.shape[0], -1, HD)
    v3 = value_part.reshape(value_part.shape[0], -1, HD)
    scores = jnp.einsum("qhd,khd->hqk", q3, k3, preferred_element_type=jnp.float32) * scale
    masked = jnp.where(allowed[None], scores, -1000000000.0)
    top = jnp.max(masked, axis=-1, keepdims=True)
    expo = jnp.exp(masked - top)
    total = jnp.sum(expo, axis=-1, keepdims=True)
    probs = (expo / total).astype(jnp.bfloat16)
    context = jnp.einsum("hqk,khd->qhd", probs, v3, preferred_element_type=jnp.float32)
    return (context.reshape(query_part.shape[0], -1), top + jnp.log(total))


def attend_back(query_part, key_part, value_part, dctx_part, lse_part, allowed):
    scale = 1.0 / math.sqrt(HD)
    q3 = query_part.reshape(query_part.shape[0], -1, HD)
    k3 = key_part.reshape(key_part.shape[0], -1, HD)
    v3 = value_part.reshape(value_part.shape[0], -1, HD)
    d3 = dctx_part.reshape(dctx_part.shape[0], -1, HD)
    scores = jnp.einsum("qhd,khd->hqk", q3, k3, preferred_element_type=jnp.float32) * scale
    masked = jnp.where(allowed[None], scores, -1000000000.0)
    probs32 = jnp.exp(masked - lse_part)
    dprobs = jnp.einsum("qhd,khd->hqk", d3, v3, preferred_element_type=jnp.float32)
    inner = jnp.sum(probs32 * dprobs, axis=-1, keepdims=True)
    dscores = (probs32 * (dprobs - inner)).astype(jnp.bfloat16)
    dquery = jnp.einsum("hqk,khd->qhd", dscores, k3, preferred_element_type=jnp.float32) * scale
    dkey = jnp.einsum("hqk,qhd->khd", dscores, q3, preferred_element_type=jnp.float32) * scale
    dvalue = jnp.einsum(
        "hqk,qhd->khd", probs32.astype(jnp.bfloat16), d3, preferred_element_type=jnp.float32
    )
    return (
        dquery.reshape(query_part.shape[0], -1),
        dkey.reshape(key_part.shape[0], -1),
        dvalue.reshape(key_part.shape[0], -1),
    )


def body(
    frames,
    segment_ids,
    row_length,
    query_proj,
    key_proj,
    value_proj,
    out_proj,
    up_proj,
    down_proj,
    query_bias,
    value_bias,
    out_bias,
    up_bias,
    down_bias,
    attn_gain,
    mlp_gain,
    out_grad,
):
    vectors = (query_bias, value_bias, out_bias, up_bias, down_bias, attn_gain, mlp_gain)
    widths = [piece.shape[0] for piece in vectors]
    packed = jnp.concatenate(vectors).reshape(1, 1, -1)
    shards = (query_proj, key_proj, value_proj, out_proj, up_proj, down_proj, packed)
    full = gather_params(shards)
    w_query, w_key, w_value, w_out, w_up, w_down = (
        full[0],
        full[1],
        full[2],
        full[3],
        full[4],
        full[5],
    )
    b_query, b_value, b_out, b_up, b_down, g_attn, g_mlp = unpack_vectors(full[6], widths)
    length = frames.shape[0]
    own_segments = segment_ids[0]
    limit = row_length[0]
    offset = lax.axis_index("narrow") * length
    frames32 = frames.astype(jnp.float32)
    act_one = rms_scale(frames32, g_attn).astype(jnp.bfloat16)
    queries = (product(act_one, w_query) + b_query).astype(jnp.bfloat16)
    keys = product(act_one, w_key).astype(jnp.bfloat16)
    values = (product(act_one, w_value) + b_value).astype(jnp.bfloat16)
    row_parts = (
        lax.all_gather(keys, "narrow", axis=0, tiled=True),
        lax.all_gather(values, "narrow", axis=0, tiled=True),
        lax.all_gather(own_segments.astype(jnp.bfloat16), "narrow", axis=0, tiled=True),
    )
    row_keys, row_values = (row_parts[0], row_parts[1])
    row_segments = row_parts[2].astype(jnp.int32)
    total = row_keys.shape[0]
    block = min(length, 512)
    starts = list(range(0, length, block))
    masks = [
        build_mask(own_segments, row_segments, limit, offset, start, block) for start in starts
    ]
    width = queries.shape[1]
    group_width = 4 * HD
    firsts = list(range(0, width, group_width))
    context_cols = []
    lse_store = []
    for first in firsts:
        key_group = row_keys[:, first : first + group_width]
        value_group = row_values[:, first : first + group_width]
        pieces = []
        lse_group = []
        for index, start in enumerate(starts):
            piece, lse_part = attend(
                queries[start : start + block, first : first + group_width],
                key_group,
                value_group,
                masks[index],
            )
            pieces.append(piece)
            lse_group.append(lse_part)
        context_cols.append(pieces[0])
        lse_store.append(lse_group)
    context = jnp.concatenate(context_cols, axis=1).astype(jnp.bfloat16)
    mid = frames32 + product(context, w_out) + b_out
    act_two = rms_scale(mid, g_mlp).astype(jnp.bfloat16)
    pre = product(act_two, w_up) + b_up
    hidden = jax.nn.gelu(pre).astype(jnp.bfloat16)
    block_out = (mid + product(hidden, w_down) + b_down).astype(jnp.bfloat16)
    again = gather_again(shards)
    w_query, w_key, w_value, w_out, w_up, w_down = (
        again[0],
        again[1],
        again[2],
        again[3],
        again[4],
        again[5],
    )
    b_query, b_value, b_out, b_up, b_down, g_attn, g_mlp = unpack_vectors(again[6], widths)
    dout32 = out_grad.astype(jnp.float32)
    down_bias_grad = jnp.sum(dout32, axis=0)
    down_grad = contract_first(hidden, out_grad)
    dhidden = contract_last(out_grad, w_down)
    _, gelu_back = jax.vjp(jax.nn.gelu, pre)
    dpre = gelu_back(dhidden)[0].astype(jnp.bfloat16)
    up_bias_grad = jnp.sum(dpre.astype(jnp.float32), axis=0)
    up_grad = contract_first(act_two, dpre)
    dact_two = contract_last(dpre, w_up)
    _, norm_two_back = jax.vjp(rms_scale, mid, g_mlp)
    dmid_norm, mlp_gain_grad = norm_two_back(dact_two)
    dmid = dout32 + dmid_norm
    dattn = dmid.astype(jnp.bfloat16)
    out_bias_grad = jnp.sum(dattn.astype(jnp.float32), axis=0)
    out_grad_w = contract_first(context, dattn)
    dcontext = contract_last(dattn, w_out).astype(jnp.bfloat16)
    dquery_cols = []
    dkey_cols = []
    dvalue_cols = []
    for group_index, first in enumerate(firsts):
        key_group = row_keys[:, first : first + group_width]
        value_group = row_values[:, first : first + group_width]
        dkey_sum = jnp.zeros((total, group_width), jnp.float32)
        dvalue_sum = jnp.zeros((total, group_width), jnp.float32)
        dquery_parts = []
        for index, start in enumerate(starts):
            dquery, dkey, dvalue = attend_back(
                queries[start : start + block, first : first + group_width],
                key_group,
                value_group,
                dcontext[start : start + block, first : first + group_width],
                lse_store[group_index][index],
                masks[index],
            )
            dquery_parts.append(dquery)
            dkey_sum = dkey
            dvalue_sum = dvalue
        dquery_cols.append(dquery_parts[0])
        dkey_cols.append(dkey_sum)
        dvalue_cols.append(dvalue_sum)
    dqueries = jnp.concatenate(dquery_cols, axis=1).astype(jnp.bfloat16)
    dkey_row = jnp.concatenate(dkey_cols, axis=1)
    dvalue_row = jnp.concatenate(dvalue_cols, axis=1)
    own_parts = (
        lax.psum_scatter(
            dkey_row.astype(jnp.bfloat16), "narrow", scatter_dimension=0, tiled=True
        ).astype(jnp.float32),
        lax.psum_scatter(
            dvalue_row.astype(jnp.bfloat16), "narrow", scatter_dimension=0, tiled=True
        ).astype(jnp.float32),
    )
    dkeys = own_parts[0].astype(jnp.bfloat16)
    dvalues = own_parts[1].astype(jnp.bfloat16)
    query_bias_grad = jnp.sum(dqueries.astype(jnp.float32), axis=0)
    value_bias_grad = jnp.sum(dvalues.astype(jnp.float32), axis=0)
    query_grad = contract_first(act_one, dqueries)
    key_grad = contract_first(act_one, dkeys)
    value_grad = contract_first(act_one, dvalues)
    dact_one = (
        contract_last(dqueries, w_query)
        + contract_last(dkeys, w_key)
        + contract_last(dvalues, w_value)
    )
    _, norm_one_back = jax.vjp(rms_scale, frames32, g_attn)
    dframes_norm, attn_gain_grad = norm_one_back(dact_one)
    frames_grad = (dmid + dframes_norm).astype(jnp.bfloat16)
    n_wide = lax.axis_size("wide")
    n_narrow = lax.axis_size("narrow")
    vector_grads = (
        query_bias_grad,
        value_bias_grad,
        out_bias_grad,
        up_bias_grad,
        down_bias_grad,
        attn_gain_grad,
        mlp_gain_grad,
    )
    columns = [
        grad.reshape(n_wide * n_narrow, width_one) for grad, width_one in zip(vector_grads, widths)
    ]
    vector_table = jnp.concatenate(columns, axis=1).reshape(n_wide, n_narrow, -1)
    section = (
        lax.psum_scatter(
            query_grad.astype(jnp.bfloat16), "narrow", scatter_dimension=1, tiled=True
        ).astype(jnp.float32),
        lax.psum_scatter(
            key_grad.astype(jnp.bfloat16), "narrow", scatter_dimension=1, tiled=True
        ).astype(jnp.float32),
        lax.psum_scatter(
            value_grad.astype(jnp.bfloat16), "narrow", scatter_dimension=1, tiled=True
        ).astype(jnp.float32),
        lax.psum_scatter(
            out_grad_w.astype(jnp.bfloat16), "narrow", scatter_dimension=1, tiled=True
        ).astype(jnp.float32),
        lax.psum_scatter(
            up_grad.astype(jnp.bfloat16), "narrow", scatter_dimension=1, tiled=True
        ).astype(jnp.float32),
        lax.psum_scatter(
            down_grad.astype(jnp.bfloat16), "narrow", scatter_dimension=1, tiled=True
        ).astype(jnp.float32),
        lax.psum_scatter(
            vector_table.astype(jnp.bfloat16), "narrow", scatter_dimension=1, tiled=True
        ).astype(jnp.float32),
    )
    final = (
        lax.psum_scatter(
            section[0].astype(jnp.bfloat16), "wide", scatter_dimension=0, tiled=True
        ).astype(jnp.float32),
        lax.psum_scatter(
            section[1].astype(jnp.bfloat16), "wide", scatter_dimension=0, tiled=True
        ).astype(jnp.float32),
        lax.psum_scatter(
            section[2].astype(jnp.bfloat16), "wide", scatter_dimension=0, tiled=True
        ).astype(jnp.float32),
        lax.psum_scatter(
            section[3].astype(jnp.bfloat16), "wide", scatter_dimension=0, tiled=True
        ).astype(jnp.float32),
        lax.psum_scatter(
            section[4].astype(jnp.bfloat16), "wide", scatter_dimension=0, tiled=True
        ).astype(jnp.float32),
        lax.psum_scatter(
            section[5].astype(jnp.bfloat16), "wide", scatter_dimension=0, tiled=True
        ).astype(jnp.float32),
        lax.psum_scatter(
            section[6].astype(jnp.bfloat16), "wide", scatter_dimension=0, tiled=True
        ).astype(jnp.float32),
    )
    flat = final[6].reshape(-1)
    split_grads = []
    offset_one = 0
    for width_one in widths:
        split_grads.append(flat[offset_one : offset_one + width_one])
        offset_one = offset_one + width_one
    return (
        block_out,
        frames_grad,
        final[0],
        final[1],
        final[2],
        final[3],
        final[4],
        final[5],
        split_grads[0],
        split_grads[1],
        split_grads[2],
        split_grads[3],
        split_grads[4],
        split_grads[5],
        split_grads[6],
    )


def plan(mesh):
    nw, nx = mesh.shape["wide"], mesh.shape["narrow"]
    if nx != 2 or nw % 4:
        return None
    return nw // 4, 2, nx


def either(parts, *args):
    d = args[0].shape[1]
    blocks = None if parts is None else parts[0] * parts[1]
    if parts is None or (d // blocks) % 128 or args[3].shape[1] % 256 or parts[0] != 2 * parts[2]:
        return body(*args)
    return fast_body(*parts, *args)


def solution(mesh):
    return jax.shard_map(
        functools.partial(either, plan(mesh)),
        mesh=mesh,
        in_specs=(
            P(("wide", "narrow"), None),
            P("wide", "narrow"),
            P("wide"),
            P("wide", "narrow"),
            P("wide", "narrow"),
            P("wide", "narrow"),
            P("wide", "narrow"),
            P("wide", "narrow"),
            P("wide", "narrow"),
            P(("wide", "narrow")),
            P(("wide", "narrow")),
            P(("wide", "narrow")),
            P(("wide", "narrow")),
            P(("wide", "narrow")),
            P(("wide", "narrow")),
            P(("wide", "narrow")),
            P(("wide", "narrow"), None),
        ),
        out_specs=(
            P(("wide", "narrow"), None),
            P(("wide", "narrow"), None),
            P("wide", "narrow"),
            P("wide", "narrow"),
            P("wide", "narrow"),
            P("wide", "narrow"),
            P("wide", "narrow"),
            P("wide", "narrow"),
            P(("wide", "narrow")),
            P(("wide", "narrow")),
            P(("wide", "narrow")),
            P(("wide", "narrow")),
            P(("wide", "narrow")),
            P(("wide", "narrow")),
            P(("wide", "narrow")),
        ),
        check_vma=False,
    )
```
